256 devices in a mesh: strip: 16 (over z_lo, y, core), tensor: 16 (over x, z_hi).
Axes of the slice: x: 4, y: 4, z: 8 (z_hi: 4, z_lo: 2; z = z_hi * 2 + z_lo), core: 2. Of those that a mesh axis runs over, the one named last changes fastest.
Arguments:
- conv_out: bfloat16 [128, 256, 1536], P('strip', 'tensor'), may hold values from -425 to 425
- out_grad: bfloat16 [128, 256, 1536], P('strip', 'tensor'), may hold values from -6 to 6
- layer_norm_gain: float32 [1536], replicated, may hold values from 0.5 to 2
- layer_norm_bias: float32 [1536], replicated, may hold values from -3 to 3
- w_in: bfloat16 [1536, 6144], P('strip', 'tensor'), may hold values from -0.15625 to 0.15625
- b_in: float32 [6144], P('tensor'), may hold values from -3 to 3
- w_out: bfloat16 [6144, 1536], P('tensor', 'strip'), may hold values from -0.078125 to 0.078125
- layer_scale: float32 [1536], replicated, may hold values from 0.25 to 2
- dw_kernel: float32 [7, 7, 1536], replicated, may hold values from -0.875 to 0.875
Outputs:
- grad_input: bfloat16 [128, 256, 1536], P('strip', 'tensor')
- grad_w_in: float32 [1536, 6144], P('strip', 'tensor')
- grad_w_out: float32 [6144, 1536], P('tensor', 'strip')
The draws below stay inside these ranges and needn't reach their ends.
All inputs are finite; a program needn't handle non-finite values.
Results may differ from the reference program's by a relative error of at most 0.0063.
Values may be sent and summed in bfloat16 or wider, within the bound.
No kernel may reach another device: no remote copies, remote signals or barrier semaphores. Data moves between devices by JAX's collectives and lax.ppermute only.
A program may use at most 128 MiB of HBM per device.

```python
import math
import jax
import jax.numpy as jnp
from jax import lax

C = 1536
HID = 6144
KSIZE = 7
IMG_ROWS = 128
IMG_COLS = 256


def draw_conv_out(key, part):
    keys = jax.random.split(key, 4)
    shape = (IMG_ROWS, IMG_COLS, C)
    base = jnp.clip(jax.random.normal(keys[0], shape, jnp.float32), -4.0, 4.0)
    row_scale = jnp.exp(jax.random.uniform(keys[1], (IMG_ROWS, IMG_COLS, 1), jnp.float32, 0.0, math.log(10.0)))
    col_scale = jnp.exp(jax.random.uniform(keys[2], (1, 1, C), jnp.float32, 0.0, math.log(10.0)))
    offset = jax.random.uniform(keys[3], (1, 1, C), jnp.float32, -2.0, 2.0)
    return (row_scale * (base * col_scale + offset)).astype(jnp.bfloat16)


def with_spikes(result, stream_key, source, target, blocks, factor):
    owner, partner = [(jnp.arange(result.shape[position]) // (result.shape[position] // blocks)).reshape([-1 if axis == position else 1 for axis in range(result.ndim)]) for position in (source, target)]
    chosen = jax.random.permutation(stream_key, blocks)[partner]
    strong = (owner == chosen) | (owner == (partner + blocks // 2) % blocks)
    return jnp.where(strong, factor * result, result)


def block_levels(rng, dims, cuts, least, high):
    gain = 1.0
    for axis_at, blocks in cuts:
        heights = jax.random.uniform(jax.random.fold_in(jax.random.fold_in(rng, 6), axis_at), (blocks,), jnp.float32, least / len(cuts), high / len(cuts))
        gain = gain * jnp.repeat(jnp.exp(heights), dims[axis_at] // blocks).reshape((-1,) + (1,) * (len(dims) - 1 - axis_at))
    return gain


def noise(stream_key, dims, deviation, limit, cuts=(), dtype=jnp.bfloat16):
    values = jax.random.normal(stream_key, dims, jnp.float32) * deviation
    if len(cuts) > 0:
        values = block_levels(stream_key, dims, cuts, -0.22, 0.18) * values
    return jnp.clip(values, min=-limit, max=limit).astype(dtype)


def bell_draw_with(own_key, dims, scale, limit, cuts, heavy, kind=jnp.bfloat16):
    array = scale * jax.random.normal(own_key, dims, jnp.float32)
    if cuts:
        array = array * block_levels(own_key, dims, cuts, -0.22, 0.18)
    return jnp.clip(with_spikes(array, jax.random.fold_in(own_key, 3), *heavy), -limit, limit).astype(kind)


def setup_inputs(seed: int = 0) -> dict:
    streams_of = jax.random.split(jax.random.key(seed), 10)
    conv_out = draw_conv_out(jax.random.fold_in(streams_of[9], 71), 0)
    out_grad = bell_draw_with(streams_of[1], (IMG_ROWS, IMG_COLS, C), 1.0, 6.0, ((0, 16), (1, 16)), (0, 2, 16, 2.0))
    layer_norm_gain = jnp.clip(jnp.exp(jax.random.uniform(streams_of[2], (C,), jnp.float32, math.log(0.5), math.log(2.0))), 0.5, 2.0)
    layer_norm_bias = noise(streams_of[3], (C,), 0.5, 3.0, (), jnp.float32)
    w_in = noise(streams_of[4], (C, HID), C ** -0.5, 0.15625, ((0, 16), (1, 16)))
    b_in = noise(streams_of[5], (HID,), 0.5, 3.0, ((0, 16),), jnp.float32)
    w_out = noise(streams_of[6], (HID, C), HID ** -0.5, 0.078125, ((0, 16), (1, 16)))
    layer_scale = jnp.clip(jnp.exp(jax.random.uniform(streams_of[7], (C,), jnp.float32, math.log(0.25), math.log(2.0))), 0.25, 2.0)
    dw_kernel = noise(streams_of[8], (KSIZE, KSIZE, C), (KSIZE * KSIZE) ** -0.5, 0.875, (), jnp.float32)
    return {"conv_out": conv_out, "out_grad": out_grad, "layer_norm_gain": layer_norm_gain, "layer_norm_bias": layer_norm_bias, "w_in": w_in, "b_in": b_in, "w_out": w_out, "layer_scale": layer_scale, "dw_kernel": dw_kernel}


ln_eps = 1e-06
root_half = 0.7071067811865476
density_norm = 0.3989422804014327

def gelu_value(value):
    return 0.5 * value * (1.0 + lax.erf(value * root_half))

def gelu_slope(value):
    return 0.5 * (1.0 + lax.erf(value * root_half)) + value * jnp.exp(-0.5 * value * value) * density_norm

def apply_layer_norm(flattened_rows):
    centre = lax.optimization_barrier(jnp.mean(flattened_rows, axis=-1, keepdims=True))
    centred = flattened_rows - centre
    spread = lax.optimization_barrier(jnp.mean(centred * centred, axis=-1, keepdims=True))
    inverse_deviation = lax.rsqrt(spread + ln_eps)
    return (centred * inverse_deviation, inverse_deviation)

def layer_norm_backward(normed_gradient, centred_input, inverse_deviation, layer_norm_gain):
    gain_scaled = normed_gradient * layer_norm_gain
    first_moment = lax.optimization_barrier(jnp.mean(gain_scaled, axis=-1, keepdims=True))
    second_moment = lax.optimization_barrier(jnp.mean(gain_scaled * centred_input, axis=-1, keepdims=True))
    return inverse_deviation * (gain_scaled - first_moment - centred_input * second_moment)

def transpose_conv(padded, dw_kernel, image_height, image_breadth):
    taps = dw_kernel.shape[0]
    total = jnp.zeros((image_height, image_breadth, padded.shape[2]), jnp.float32)
    for row_tap in range(taps):
        for col_tap in range(taps):
            start_row = taps - 1 - row_tap
            start_col = taps - 1 - col_tap
            total = total + dw_kernel[row_tap, col_tap] * padded[start_row:start_row + image_height, start_col:start_col + image_breadth]
    return total

def reference(conv_out, out_grad, layer_norm_gain, layer_norm_bias, w_in, b_in, w_out, layer_scale, dw_kernel):
    image_height, image_breadth, channel_count = conv_out.shape
    count = image_height * image_breadth
    hidden = w_in.shape[1]
    flattened_rows = conv_out.astype(jnp.float32).reshape(count, channel_count)
    centred_input, inverse_deviation = apply_layer_norm(flattened_rows)
    normed_output = (centred_input * layer_norm_gain + layer_norm_bias).astype(jnp.bfloat16)
    upstream = out_grad.astype(jnp.float32).reshape(count, channel_count)
    scaled_grad = (upstream * layer_scale).astype(jnp.bfloat16)
    block = math.gcd(count, 4096)

    def advance(carry, pieces):
        grad_in, grad_out = carry
        normed_blk, scaled_blk = pieces
        pre_act = jnp.dot(normed_blk, w_in, preferred_element_type=jnp.float32) + b_in
        hidden_act = gelu_value(pre_act).astype(jnp.bfloat16)
        back_act = lax.dot_general(scaled_blk, w_out, (((1,), (1,)), ((), ())), preferred_element_type=jnp.float32)
        back_pre = (back_act * gelu_slope(pre_act)).astype(jnp.bfloat16)
        grad_in = grad_in + lax.dot_general(normed_blk, back_pre, (((0,), (0,)), ((), ())), preferred_element_type=jnp.float32)
        grad_out = grad_out + lax.dot_general(hidden_act, scaled_blk, (((0,), (0,)), ((), ())), preferred_element_type=jnp.float32)
        normed_gradient = lax.dot_general(back_pre, w_in, (((1,), (1,)), ((), ())), preferred_element_type=jnp.float32)
        return ((grad_in, grad_out), normed_gradient)
    start = (jnp.zeros((channel_count, hidden), jnp.float32), jnp.zeros((hidden, channel_count), jnp.float32))
    (grad_in, grad_out), normed_gradient = lax.scan(advance, start, (normed_output.reshape(-1, block, channel_count), scaled_grad.reshape(-1, block, channel_count)))
    normed_gradient = normed_gradient.reshape(count, channel_count)
    factor = 1.0 / math.sqrt(count)
    convolution_gradient = layer_norm_backward(normed_gradient, centred_input, inverse_deviation, layer_norm_gain).astype(jnp.bfloat16).reshape(image_height, image_breadth, channel_count)
    margin = dw_kernel.shape[0] // 2
    padded = jnp.pad(convolution_gradient.astype(jnp.float32), ((margin, margin), (margin, margin), (0, 0)))
    grad_input = (upstream.reshape(image_height, image_breadth, channel_count) + transpose_conv(padded, dw_kernel, image_height, image_breadth)).astype(jnp.bfloat16)
    return (grad_input, grad_in * factor, grad_out * factor)
```

```python
import functools
import math

import jax
import jax.numpy as jnp
from jax import lax
from jax.experimental import pallas as pl
from jax.experimental.pallas import tpu as pltpu
from jax.sharding import Mesh
from jax.sharding import PartitionSpec as P

ln_eps = 1e-06
root_half = 0.7071067811865476
density_norm = 0.3989422804014327

FINE = ("zl", "y", "c", "x", "zh")
SIZES = (2, 4, 2, 4, 4)
STRIP = ("zl", "y", "c")
TENSOR = ("x", "zh")
Z = ("zl", "zh")
NX, NY, NZ = 4, 4, 8
CHAN, HIDDEN = 1536, 1536
ROWS, COLS = 96, 384
AY, BY = 32, 64
BLOCK = 128
TOKENS = BLOCK * NX

bf16, f32 = jnp.bfloat16, jnp.float32


def z_index(z):
    return (z % 2) * (NZ // 2) + z // 2


def z_shift(k):
    return [(z_index(z), z_index((z + k) % NZ)) for z in range(NZ)]


def shift(n, k):
    return [(i, (i + k) % n) for i in range(n)]


def to_x(value, k):
    return lax.ppermute(value, "x", shift(NX, k)) if k else value


def to_y(value, k):
    return lax.ppermute(value, "y", shift(NY, k)) if k else value


def to_z(value, k):
    return lax.ppermute(value, Z, z_shift(k)) if k else value


def swap(value):
    return lax.ppermute(value, "c", shift(2, 1))


def with_halo(block, sides, width):
    for axis, dim in sides:
        count = lax.axis_size(axis)
        forward = [(i, i + 1) for i in range(count - 1)]
        backward = [(target, source) for source, target in forward]
        low = lax.ppermute(
            lax.slice_in_dim(block, block.shape[dim] - width, None, axis=dim), axis, forward
        )
        high = lax.ppermute(lax.slice_in_dim(block, 0, width, axis=dim), axis, backward)
        block = jnp.concatenate([low, block, high], axis=dim)
    return block


def apply_layer_norm(flattened_rows):
    centre = jnp.mean(flattened_rows, axis=-1, keepdims=True)
    centred = flattened_rows - centre
    spread = jnp.mean(centred * centred, axis=-1, keepdims=True)
    inverse_deviation = lax.rsqrt(spread + ln_eps)
    return (centred * inverse_deviation, inverse_deviation)


def layer_norm_backward(normed_gradient, centred_input, inverse_deviation, layer_norm_gain):
    gain_scaled = normed_gradient * layer_norm_gain
    first_moment = jnp.mean(gain_scaled, axis=-1, keepdims=True)
    second_moment = jnp.mean(gain_scaled * centred_input, axis=-1, keepdims=True)
    return inverse_deviation * (gain_scaled - first_moment - centred_input * second_moment)


def transpose_conv(padded, dw_kernel, image_height, image_breadth):
    taps = dw_kernel.shape[0]
    total = jnp.zeros((image_height, image_breadth, padded.shape[2]), jnp.float32)
    for row_tap in range(taps):
        for col_tap in range(taps):
            start_row = taps - 1 - row_tap
            start_col = taps - 1 - col_tap
            total = (
                total
                + dw_kernel[row_tap, col_tap]
                * padded[
                    start_row : start_row + image_height, start_col : start_col + image_breadth
                ]
            )
    return total


def place(where, d, k, r):
    y, z, c = where[0], where[1], where[2]
    zz = lax.rem(z + k, NZ)
    row = (lax.rem(zz, 2) * 8 + lax.rem(y + r, NY) * 2 + (lax.rem(c + d, 2))) * ROWS
    col = (zz // 2) * COLS
    return pl.multiple_of(row, 32), pl.multiple_of(col, 128)


def compute_kernel(where, *refs):
    n = 0

    def take(count):
        nonlocal n
        n += count
        return refs[n - count : n]

    bias = take(1)[0]
    tok = take(NX)
    first = [take(NZ), take(NZ)]
    second = [take(NY), take(NY)]
    out_y = take(2)
    out_z = take(2)
    gn = take(NX)
    w, xs, xt, acts, g = take(5)
    for i in range(NX):
        rows = slice(i * BLOCK, (i + 1) * BLOCK)
        xs[0, rows, :] = tok[i][:BLOCK]
        xs[1, rows, :] = tok[i][BLOCK:]
    for d in range(2):
        for k in range(NZ):
            for r in range(NY):
                row, col = place(where, d, k, r)
                for m in range(2):
                    w[m, pl.ds(row, AY), pl.ds(col, COLS)] = first[d][k][
                        r * 2 * AY + m * AY : r * 2 * AY + m * AY + AY, :
                    ]
                    row2 = pl.multiple_of(row + AY, 32)
                    w[m, pl.ds(row2, BY), pl.ds(col, COLS)] = second[d][r][
                        k * 2 * BY + m * BY : k * 2 * BY + m * BY + BY, :
                    ]
    for m in range(2):
        for i in range(CHAN // 256):
            xt[m, i * 256 : (i + 1) * 256, :] = xs[m, :, i * 256 : (i + 1) * 256].T

    width = 256

    def activations(i, _):
        cols = pl.ds(pl.multiple_of(i * width, width), width)
        pre = jnp.dot(xs[0], w[0, :, cols], preferred_element_type=f32) + bias[:, cols]
        back = jnp.dot(xs[1], w[1, :, cols], preferred_element_type=f32)
        cdf = 0.5 * (1.0 + lax.erf(pre * root_half))
        slope = cdf + pre * jnp.exp(-0.5 * pre * pre) * density_norm
        act = (pre * cdf).astype(bf16)
        acts[:, cols] = (back * slope).astype(bf16)
        g[:, cols] = jnp.dot(xt[1], act, preferred_element_type=f32).astype(bf16)
        return 0

    def flush(m):
        for d in range(2):
            for k in range(NZ):
                for r in range(NY):
                    row, col = place(where, d, k, r)
                    row2 = pl.multiple_of(row + AY, 32)
                    out_z[d][k, r, m] = g[pl.ds(row, AY), pl.ds(col, COLS)]
                    out_y[d][r, k, m] = g[pl.ds(row2, BY), pl.ds(col, COLS)]

    lax.fori_loop(0, HIDDEN // width, activations, 0)
    flush(1)

    def gradient_in(i, _):
        cols = pl.ds(pl.multiple_of(i * width, width), width)
        g[:, cols] = jnp.dot(xt[0], acts[:, cols], preferred_element_type=f32).astype(bf16)
        return 0

    lax.fori_loop(0, HIDDEN // width, gradient_in, 0)
    flush(0)

    def gradient_normed(i, _):
        cols = pl.ds(pl.multiple_of(i * width, width), width)
        part = lax.dot_general(
            acts[...], w[0, cols, :], (((1,), (1,)), ((), ())), preferred_element_type=f32
        ).astype(bf16)
        for b in range(NX):
            gn[b][:, cols] = part[b * BLOCK : (b + 1) * BLOCK]
        return 0

    lax.fori_loop(0, CHAN // width, gradient_normed, 0)


def compute(where, bias, tok, first, second):
    vmem = pl.BlockSpec(memory_space=pltpu.VMEM)
    gy = jax.ShapeDtypeStruct((NY, NZ, 2, BY, COLS), bf16)
    gz = jax.ShapeDtypeStruct((NZ, NY, 2, AY, COLS), bf16)
    gn = jax.ShapeDtypeStruct((BLOCK, CHAN), bf16)
    operands = [bias, *tok, *first[0], *first[1], *second[0], *second[1]]
    out = pl.pallas_call(
        compute_kernel,
        out_shape=[gy, gy, gz, gz] + [gn] * NX,
        in_specs=[pl.BlockSpec(memory_space=pltpu.SMEM)] + [vmem] * len(operands),
        out_specs=[vmem] * (4 + NX),
        scratch_shapes=[
            pltpu.VMEM((2, CHAN, HIDDEN), bf16),
            pltpu.VMEM((2, TOKENS, CHAN), bf16),
            pltpu.VMEM((2, CHAN, TOKENS), bf16),
            pltpu.VMEM((TOKENS, HIDDEN), bf16),
            pltpu.VMEM((CHAN, HIDDEN), bf16),
        ],
        compiler_params=pltpu.CompilerParams(vmem_limit_bytes=60 * 2**20),
        cost_estimate=pl.CostEstimate(
            flops=10 * TOKENS * CHAN * HIDDEN, bytes_accessed=25_000_000, transcendentals=0
        ),
        name="block",
    )(where, *operands)
    return out[0:2], out[2:4], out[4:]


def add_kernel(*refs):
    own_y, got_y, own_z, got_z = refs[:4]
    ys, zs = refs[4 : 4 + NY], refs[4 + NY :]
    for r in range(NY):
        for k in range(NZ):
            ys[r][k] = (own_y[r, k].astype(f32) + got_y[r, k].astype(f32)).astype(bf16)
    for k in range(NZ):
        for r in range(NY):
            zs[k][r] = (own_z[k, r].astype(f32) + got_z[k, r].astype(f32)).astype(bf16)


def add_cores(own_y, got_y, own_z, got_z):
    vmem = pl.BlockSpec(memory_space=pltpu.VMEM)
    out = pl.pallas_call(
        add_kernel,
        out_shape=[jax.ShapeDtypeStruct(own_y.shape[1:], bf16)] * NY
        + [jax.ShapeDtypeStruct(own_z.shape[1:], bf16)] * NZ,
        in_specs=[vmem] * 4,
        out_specs=[vmem] * (NY + NZ),
        compiler_params=pltpu.CompilerParams(vmem_limit_bytes=40 * 2**20),
        name="add_cores",
    )(own_y, got_y, own_z, got_z)
    return out[:NY], out[NY:]


def sum_kernel(count, *refs):
    outs = refs[count:]
    for i, out in enumerate(outs):
        total = refs[0][i].astype(f32)
        for ref in refs[1:count]:
            total = total + ref[i].astype(f32)
        out[...] = total.astype(out.dtype)


def sum_parts(parts):
    vmem = pl.BlockSpec(memory_space=pltpu.VMEM)
    shape = parts[0].shape
    return pl.pallas_call(
        functools.partial(sum_kernel, len(parts)),
        out_shape=[jax.ShapeDtypeStruct(shape[1:], bf16)] * shape[0],
        in_specs=[vmem] * len(parts),
        out_specs=[vmem] * shape[0],
        compiler_params=pltpu.CompilerParams(vmem_limit_bytes=24 * 2**20),
        name="sum_parts",
    )(*parts)


def total(parts):
    result = parts[0].astype(f32)
    for part in parts[1:]:
        result = result + part.astype(f32)
    return result


def body(
    conv_out, out_grad, layer_norm_gain, layer_norm_bias, w_in, b_in, w_out, layer_scale, dw_kernel
):
    tile_rows, tile_cols, channel_count = conv_out.shape
    local_count = tile_rows * tile_cols
    w_out_t = w_out.T
    lead = jnp.concatenate([w_in[:AY], w_out_t[:AY]])
    rest = jnp.concatenate([w_in[AY:], w_out_t[AY:]])
    rest_z = jnp.concatenate([to_z(rest, -k) for k in range(NZ)])
    lead_y = jnp.concatenate([to_y(lead, -r) for r in range(NY)])
    second = [to_y(rest_z, -r) for r in range(NY)]
    first = [to_z(lead_y, -k) for k in range(NZ)]
    second = [second, [swap(v) for v in second]]
    first = [first, [swap(v) for v in first]]
    bias = lax.all_gather(b_in, "zh", axis=0, tiled=True).reshape(1, HIDDEN)

    flattened_rows = conv_out.astype(jnp.float32).reshape(local_count, channel_count)
    centred_input, inverse_deviation = apply_layer_norm(flattened_rows)
    normed_output = (centred_input * layer_norm_gain + layer_norm_bias).astype(jnp.bfloat16)
    upstream = out_grad.astype(jnp.float32)
    scaled_grad = (upstream.reshape(local_count, channel_count) * layer_scale).astype(jnp.bfloat16)
    token = jnp.concatenate([normed_output, scaled_grad])
    tok = [to_x(token, -r) for r in range(NX)]

    where = jnp.stack(
        [lax.axis_index("y"), lax.axis_index("zh") * 2 + lax.axis_index("zl"), lax.axis_index("c")]
    ).astype(jnp.int32)
    grad_y, grad_z, part = compute(where, bias, tok, first, second)

    normed_gradient = total([to_x(v, r) for r, v in enumerate(part)])

    ys, zs = add_cores(grad_y[0], swap(grad_y[1]), grad_z[0], swap(grad_z[1]))
    zs = [to_z(v, k) for k, v in enumerate(zs)]
    ys = [to_y(v, r) for r, v in enumerate(ys)]
    ys = sum_parts(ys)
    ys = [to_z(v, k) for k, v in enumerate(ys)]
    zs = sum_parts(zs)
    zs = [to_y(v, r) for r, v in enumerate(zs)]
    total_tokens = local_count * lax.axis_size(STRIP) * lax.axis_size(TENSOR)
    factor = 1.0 / math.sqrt(total_tokens)
    summed = jnp.concatenate([total(zs), total(ys)], axis=1) * factor

    convolution_gradient = (
        layer_norm_backward(normed_gradient, centred_input, inverse_deviation, layer_norm_gain)
        .astype(jnp.bfloat16)
        .reshape(tile_rows, tile_cols, channel_count)
    )
    margin = dw_kernel.shape[0] // 2
    padded = with_halo(convolution_gradient, ((STRIP, 0), (TENSOR, 1)), margin)
    grad_input = (
        upstream + transpose_conv(padded.astype(jnp.float32), dw_kernel, tile_rows, tile_cols)
    ).astype(jnp.bfloat16)
    return (grad_input, summed[0], summed[1].T)


def solution(mesh):
    fine = Mesh(mesh.devices.reshape(SIZES), FINE)
    token = P(STRIP, TENSOR, None)
    return jax.shard_map(
        body,
        mesh=fine,
        in_specs=(
            token,
            token,
            P(),
            P(),
            P(STRIP, TENSOR),
            P(TENSOR),
            P(TENSOR, STRIP),
            P(),
            P(),
        ),
        out_specs=(token, P(STRIP, TENSOR), P(TENSOR, STRIP)),
        check_vma=False,
    )
```

```python
import math

import jax
import jax.numpy as jnp
from jax import lax
from jax.experimental import pallas as pl
from jax.experimental.pallas import tpu as pltpu
from jax.sharding import Mesh
from jax.sharding import PartitionSpec as P

ln_eps = 1e-06
root_half = 0.7071067811865476
density_norm = 0.3989422804014327

FINE = ("zl", "y", "c", "x", "zh")
SIZES = (2, 4, 2, 4, 4)
STRIP = ("zl", "y", "c")
TENSOR = ("x", "zh")
Z = ("zl", "zh")
NX, NY, NZ = 4, 4, 8
CHAN, HIDDEN = 1536, 1536
ROWS, COLS = 96, 384
AY, BY = 32, 64
BLOCK = 128
TOKENS = BLOCK * NX

bf16, f32 = jnp.bfloat16, jnp.float32


def shift(n, k):
    return [(i, (i + k) % n) for i in range(n)]


def to_x(value, k):
    return lax.ppermute(value, "x", shift(NX, k)) if k else value


def to_y(value, k):
    return lax.ppermute(value, "y", shift(NY, k)) if k else value


def exchange_z(value):
    return lax.all_to_all(value, Z, 0, 0, tiled=True)


def gather_bias(value):
    parts = [lax.ppermute(value, "zh", shift(4, -q)) if q else value for q in range(4)]
    twice = jnp.stack(parts + parts)
    start = lax.rem(4 - lax.axis_index("zh"), 4)
    return lax.dynamic_slice_in_dim(twice, start, 4, 0).reshape(1, HIDDEN)


def gather_z(value):
    return exchange_z(jnp.broadcast_to(value, (NZ, *value.shape)))


def swap(value):
    return lax.ppermute(value, "c", shift(2, 1))


def with_halo(block, sides, width):
    for axis, dim in sides:
        count = lax.axis_size(axis)
        forward = [(i, i + 1) for i in range(count - 1)]
        backward = [(target, source) for source, target in forward]
        low = lax.ppermute(
            lax.slice_in_dim(block, block.shape[dim] - width, None, axis=dim), axis, forward
        )
        high = lax.ppermute(lax.slice_in_dim(block, 0, width, axis=dim), axis, backward)
        block = jnp.concatenate([low, block, high], axis=dim)
    return block


def apply_layer_norm(flattened_rows):
    centre = jnp.mean(flattened_rows, axis=-1, keepdims=True)
    centred = flattened_rows - centre
    spread = jnp.mean(centred * centred, axis=-1, keepdims=True)
    inverse_deviation = lax.rsqrt(spread + ln_eps)
    return (centred * inverse_deviation, inverse_deviation)


def layer_norm_backward(normed_gradient, centred_input, inverse_deviation, layer_norm_gain):
    gain_scaled = normed_gradient * layer_norm_gain
    first_moment = jnp.mean(gain_scaled, axis=-1, keepdims=True)
    second_moment = jnp.mean(gain_scaled * centred_input, axis=-1, keepdims=True)
    return inverse_deviation * (gain_scaled - first_moment - centred_input * second_moment)


def transpose_conv(padded, dw_kernel, image_height, image_breadth):
    taps = dw_kernel.shape[0]
    total = jnp.zeros((image_height, image_breadth, padded.shape[2]), jnp.float32)
    for row_tap in range(taps):
        for col_tap in range(taps):
            start_row = taps - 1 - row_tap
            start_col = taps - 1 - col_tap
            total = (
                total
                + dw_kernel[row_tap, col_tap]
                * padded[
                    start_row : start_row + image_height, start_col : start_col + image_breadth
                ]
            )
    return total


def place(where, d, k, r):
    y, c = where[0], where[1]
    row = (k // 4 * 8 + lax.rem(y + r, NY) * 2 + lax.rem(c + d, 2)) * ROWS
    return pl.multiple_of(row, 32), slice(k % 4 * COLS, k % 4 * COLS + COLS)


def compute_kernel(where, *refs):
    n = 0

    def take(count):
        nonlocal n
        n += count
        return refs[n - count : n]

    bias = take(1)[0]
    tok = take(NX)
    first = take(2)
    second = [take(NY), take(NY)]
    out_y = take(2)
    out_z = take(2)
    gn = take(NX)
    w, xs, xt, acts, g = take(5)
    for i in range(NX):
        rows = slice(i * BLOCK, (i + 1) * BLOCK)
        xs[0, rows, :] = tok[i][:BLOCK]
        xs[1, rows, :] = tok[i][BLOCK:]
    for d in range(2):
        for k in range(NZ):
            for r in range(NY):
                row, col = place(where, d, k, r)
                for m in range(2):
                    row2 = pl.multiple_of(row + AY, 32)
                    w[m, pl.ds(row, AY), col] = first[d][k, r, m]
                    w[m, pl.ds(row2, BY), col] = second[d][r][k, m]
    for m in range(2):
        for i in range(CHAN // 256):
            xt[m, i * 256 : (i + 1) * 256, :] = xs[m, :, i * 256 : (i + 1) * 256].T

    width = 256

    def activations(i, _):
        cols = pl.ds(pl.multiple_of(i * width, width), width)
        pre = jnp.dot(xs[0], w[0, :, cols], preferred_element_type=f32) + bias[:, cols]
        back = jnp.dot(xs[1], w[1, :, cols], preferred_element_type=f32)
        cdf = 0.5 * (1.0 + lax.erf(pre * root_half))
        slope = cdf + pre * jnp.exp(-0.5 * pre * pre) * density_norm
        act = (pre * cdf).astype(bf16)
        acts[:, cols] = (back * slope).astype(bf16)
        g[:, cols] = jnp.dot(xt[1], act, preferred_element_type=f32).astype(bf16)
        return 0

    def flush(m):
        for d in range(2):
            for k in range(NZ):
                for r in range(NY):
                    row, col = place(where, d, k, r)
                    row2 = pl.multiple_of(row + AY, 32)
                    out_z[d][k, r, m] = g[pl.ds(row, AY), col]
                    out_y[d][r, k, m] = g[pl.ds(row2, BY), col]

    lax.fori_loop(0, HIDDEN // width, activations, 0)
    flush(1)

    def gradient_in(i, _):
        cols = pl.ds(pl.multiple_of(i * width, width), width)
        g[:, cols] = jnp.dot(xt[0], acts[:, cols], preferred_element_type=f32).astype(bf16)
        return 0

    lax.fori_loop(0, HIDDEN // width, gradient_in, 0)
    flush(0)

    def gradient_normed(i, _):
        cols = pl.ds(pl.multiple_of(i * width, width), width)
        part = lax.dot_general(
            acts[...], w[0, cols, :], (((1,), (1,)), ((), ())), preferred_element_type=f32
        ).astype(bf16)
        for b in range(NX):
            gn[b][:, cols] = part[b * BLOCK : (b + 1) * BLOCK]
        return 0

    lax.fori_loop(0, CHAN // width, gradient_normed, 0)


def compute(where, bias, tok, first, second):
    vmem = pl.BlockSpec(memory_space=pltpu.VMEM)
    gy = jax.ShapeDtypeStruct((NY, NZ, 2, BY, COLS), bf16)
    gz = jax.ShapeDtypeStruct((NZ, NY, 2, AY, COLS), bf16)
    gn = jax.ShapeDtypeStruct((BLOCK, CHAN), bf16)
    operands = [bias, *tok, *first, *second[0], *second[1]]
    out = pl.pallas_call(
        compute_kernel,
        out_shape=[gy, gy, gz, gz] + [gn] * NX,
        in_specs=[pl.BlockSpec(memory_space=pltpu.SMEM)] + [vmem] * len(operands),
        out_specs=[vmem] * (4 + NX),
        scratch_shapes=[
            pltpu.VMEM((2, CHAN, HIDDEN), bf16),
            pltpu.VMEM((2, TOKENS, CHAN), bf16),
            pltpu.VMEM((2, CHAN, TOKENS), bf16),
            pltpu.VMEM((TOKENS, HIDDEN), bf16),
            pltpu.VMEM((CHAN, HIDDEN), bf16),
        ],
        compiler_params=pltpu.CompilerParams(vmem_limit_bytes=60 * 2**20),
        cost_estimate=pl.CostEstimate(
            flops=10 * TOKENS * CHAN * HIDDEN, bytes_accessed=25_000_000, transcendentals=0
        ),
        name="block",
    )(where, *operands)
    return out[0:2], out[2:4], out[4:]


def add_kernel(*refs):
    own_y, got_y, own_z, got_z = refs[:4]
    ys, zs = refs[4 : 4 + NY], refs[4 + NY]
    for r in range(NY):
        for k in range(NZ):
            ys[r][k] = (own_y[r, k].astype(f32) + got_y[r, k].astype(f32)).astype(bf16)
    for k in range(NZ):
        for r in range(NY):
            zs[k, r] = (own_z[k, r].astype(f32) + got_z[k, r].astype(f32)).astype(bf16)


def add_cores(own_y, got_y, own_z, got_z):
    vmem = pl.BlockSpec(memory_space=pltpu.VMEM)
    out = pl.pallas_call(
        add_kernel,
        out_shape=[jax.ShapeDtypeStruct(own_y.shape[1:], bf16)] * NY
        + [jax.ShapeDtypeStruct(own_z.shape, bf16)],
        in_specs=[vmem] * 4,
        out_specs=[vmem] * (NY + 1),
        compiler_params=pltpu.CompilerParams(vmem_limit_bytes=40 * 2**20),
        name="add_cores",
    )(own_y, got_y, own_z, got_z)
    return out[:NY], out[NY]


def sum_y_kernel(*refs):
    for k in range(NZ):
        total = refs[0][k].astype(f32)
        for ref in refs[1:NY]:
            total = total + ref[k].astype(f32)
        refs[NY][k] = total.astype(bf16)


def sum_y(parts):
    vmem = pl.BlockSpec(memory_space=pltpu.VMEM)
    return pl.pallas_call(
        sum_y_kernel,
        out_shape=jax.ShapeDtypeStruct(parts[0].shape, bf16),
        in_specs=[vmem] * NY,
        out_specs=vmem,
        compiler_params=pltpu.CompilerParams(vmem_limit_bytes=24 * 2**20),
        name="sum_y",
    )(*parts)


def sum_z_kernel(parts, *outs):
    for r in range(NY):
        total = parts[0, r].astype(f32)
        for k in range(1, NZ):
            total = total + parts[k, r].astype(f32)
        outs[r][...] = total.astype(bf16)


def sum_z(parts):
    vmem = pl.BlockSpec(memory_space=pltpu.VMEM)
    return pl.pallas_call(
        sum_z_kernel,
        out_shape=[jax.ShapeDtypeStruct(parts.shape[2:], bf16)] * NY,
        in_specs=[vmem],
        out_specs=[vmem] * NY,
        compiler_params=pltpu.CompilerParams(vmem_limit_bytes=24 * 2**20),
        name="sum_z",
    )(parts)


def total(parts):
    result = parts[0].astype(f32)
    for part in parts[1:]:
        result = result + part.astype(f32)
    return result


def body(
    conv_out, out_grad, layer_norm_gain, layer_norm_bias, w_in, b_in, w_out, layer_scale, dw_kernel
):
    tile_rows, tile_cols, channel_count = conv_out.shape
    local_count = tile_rows * tile_cols
    flattened_rows = conv_out.astype(jnp.float32).reshape(local_count, channel_count)
    centred_input, inverse_deviation = apply_layer_norm(flattened_rows)
    normed_output = (centred_input * layer_norm_gain + layer_norm_bias).astype(jnp.bfloat16)
    upstream = out_grad.astype(jnp.float32)
    scaled_grad = (upstream.reshape(local_count, channel_count) * layer_scale).astype(jnp.bfloat16)
    token = jnp.concatenate([normed_output, scaled_grad])
    tok = [to_x(token, -r) for r in range(NX)]

    shards = jnp.stack([w_in, w_out.T])
    lead, rest = shards[:, :AY], shards[:, AY:]
    rest_z = gather_z(rest)
    lead_y = jnp.stack([to_y(lead, -r) for r in range(NY)])
    bias = gather_bias(b_in)
    rest_z, lead_y, bias, tok[1], tok[3] = lax.optimization_barrier(
        (rest_z, lead_y, bias, tok[1], tok[3])
    )
    second = [to_y(rest_z, -r) for r in range(NY)]
    first = gather_z(lead_y)
    second = [second, [swap(v) for v in second]]
    first = [first, swap(first)]

    where = jnp.stack([lax.axis_index("y"), lax.axis_index("c")]).astype(jnp.int32)
    grad_y, grad_z, part = compute(where, bias, tok, first, second)

    ys, zs = add_cores(grad_y[0], swap(grad_y[1]), grad_z[0], swap(grad_z[1]))
    ys, part = list(ys), list(part)
    ys[0], part[2] = lax.optimization_barrier((ys[0], part[2]))
    part = [to_x(v, r) for r, v in enumerate(part)]
    ys = [to_y(v, r) for r, v in enumerate(ys)]
    part[0], ys[1], ys[3] = lax.optimization_barrier((part[0], ys[1], ys[3]))
    normed_gradient = total(part)

    ys = sum_y(ys)
    zs = sum_z(exchange_z(zs))
    zs = [to_y(v, r) for r, v in enumerate(zs)]
    ys = exchange_z(ys)
    total_tokens = local_count * lax.axis_size(STRIP) * lax.axis_size(TENSOR)
    factor = 1.0 / math.sqrt(total_tokens)
    summed = jnp.concatenate([total(zs), total(ys)], axis=1) * factor

    convolution_gradient = (
        layer_norm_backward(normed_gradient, centred_input, inverse_deviation, layer_norm_gain)
        .astype(jnp.bfloat16)
        .reshape(tile_rows, tile_cols, channel_count)
    )
    margin = dw_kernel.shape[0] // 2
    padded = with_halo(convolution_gradient, ((STRIP, 0), (TENSOR, 1)), margin)
    grad_input = (
        upstream + transpose_conv(padded.astype(jnp.float32), dw_kernel, tile_rows, tile_cols)
    ).astype(jnp.bfloat16)
    return (grad_input, summed[0], summed[1].T)


def solution(mesh):
    fine = Mesh(mesh.devices.reshape(SIZES), FINE)
    token = P(STRIP, TENSOR, None)
    return jax.shard_map(
        body,
        mesh=fine,
        in_specs=(
            token,
            token,
            P(),
            P(),
            P(STRIP, TENSOR),
            P(TENSOR),
            P(TENSOR, STRIP),
            P(),
            P(),
        ),
        out_specs=(token, P(STRIP, TENSOR), P(TENSOR, STRIP)),
        check_vma=False,
    )
```

```python
import math

import jax
import jax.numpy as jnp
from jax import lax
from jax.experimental import pallas as pl
from jax.experimental.pallas import tpu as pltpu
from jax.sharding import Mesh
from jax.sharding import PartitionSpec as P

ln_eps = 1e-06
root_half = 0.7071067811865476
density_norm = 0.3989422804014327

FINE = ("zl", "y", "c", "x", "zh")
SIZES = (2, 4, 2, 4, 4)
STRIP = ("zl", "y", "c")
TENSOR = ("x", "zh")
Z = ("zl", "zh")
NX, NY, NZ = 4, 4, 8
CHAN, HIDDEN = 1536, 1536
ROWS, COLS = 96, 384
AY, BY = 32, 64
BLOCK = 128
TOKENS = BLOCK * NX

bf16, f32 = jnp.bfloat16, jnp.float32


def shift(n, k):
    return [(i, (i + k) % n) for i in range(n)]


def to_x(value, k):
    return lax.ppermute(value, "x", shift(NX, k)) if k else value


def to_y(value, k):
    return lax.ppermute(value, "y", shift(NY, k)) if k else value


def exchange_z(value):
    return lax.all_to_all(value, Z, 0, 0, tiled=True)


def bias_rows(bias):
    rows = []
    for _ in range(3):
        term = lax.reduce_precision(bias, 8, 7)
        rows.append(term.astype(bf16))
        bias = bias - term
    return jnp.concatenate([jnp.stack(rows), jnp.zeros((13, COLS), bf16)])


def gather_z(value):
    return exchange_z(jnp.broadcast_to(value, (NZ, *value.shape)))


def swap(value):
    return lax.ppermute(value, "c", shift(2, 1))


HALO = (
    (1, 0, slice(5, 8), slice(0, 16)),
    (-1, 0, slice(0, 3), slice(0, 16)),
    (0, 1, slice(0, 8), slice(13, 16)),
    (0, -1, slice(0, 8), slice(0, 3)),
    (1, 1, slice(5, 8), slice(13, 16)),
    (1, -1, slice(5, 8), slice(0, 3)),
    (-1, 1, slice(0, 3), slice(13, 16)),
    (-1, -1, slice(0, 3), slice(0, 3)),
)
TILE_ROWS, TILE_COLS, TAPS, MARGIN = 8, 16, 7, 3


def to_tile(value, down, right):
    pairs = [
        (s * 16 + t, (s + down) * 16 + t + right)
        for s in range(16)
        for t in range(16)
        if 0 <= s + down < 16 and 0 <= t + right < 16
    ]
    return lax.ppermute(value, FINE, pairs)


def vmem_specs(count):
    return [pl.BlockSpec(memory_space=pltpu.VMEM)] * count


def norm_kernel(x, grad, gain, bias, scale, token, xhat, inverse):
    for i in range(0, BLOCK, 16):
        rows = slice(i, i + 16)
        value = x[rows].astype(f32)
        value = value - jnp.mean(value, axis=-1, keepdims=True)
        inv = lax.rsqrt(jnp.mean(value * value, axis=-1, keepdims=True) + ln_eps)
        value = value * inv
        xhat[rows] = value
        inverse[rows] = inv
        token[rows] = (value * gain[...] + bias[...]).astype(bf16)
        token[i + BLOCK : i + BLOCK + 16] = (grad[rows].astype(f32) * scale[...]).astype(bf16)


def layer_norm(x, grad, gain, bias, scale):
    return pl.pallas_call(
        norm_kernel,
        out_shape=[
            jax.ShapeDtypeStruct((2 * BLOCK, CHAN), bf16),
            jax.ShapeDtypeStruct((BLOCK, CHAN), f32),
            jax.ShapeDtypeStruct((BLOCK, 1), f32),
        ],
        in_specs=vmem_specs(5),
        out_specs=vmem_specs(3),
        compiler_params=pltpu.CompilerParams(vmem_limit_bytes=16 * 2**20),
        name="layer_norm",
    )(x, grad, gain, bias, scale)


def norm_backward_kernel(*refs):
    parts, (xhat, inverse, gain, out), halos = refs[:NX], refs[NX : NX + 4], refs[NX + 4 :]
    for i in range(TILE_ROWS):
        rows = slice(i * TILE_COLS, (i + 1) * TILE_COLS)
        value = parts[0][rows].astype(f32)
        for part in parts[1:]:
            value = value + part[rows].astype(f32)
        value = value * gain[...]
        hat = xhat[rows]
        first = jnp.mean(value, axis=-1, keepdims=True)
        second = jnp.mean(value * hat, axis=-1, keepdims=True)
        value = inverse[rows] * (value - first - hat * second)
        out[i] = value.astype(bf16)
        for (_, _, height, breadth), halo in zip(HALO, halos, strict=True):
            if height.start <= i < height.stop:
                halo[i - height.start] = value[breadth].astype(bf16)


def layer_norm_backward(parts, xhat, inverse, gain):
    return pl.pallas_call(
        norm_backward_kernel,
        out_shape=[jax.ShapeDtypeStruct((TILE_ROWS, TILE_COLS, CHAN), bf16)]
        + [
            jax.ShapeDtypeStruct((h.stop - h.start, b.stop - b.start, CHAN), bf16)
            for _, _, h, b in HALO
        ],
        in_specs=vmem_specs(NX + 3),
        out_specs=vmem_specs(9),
        compiler_params=pltpu.CompilerParams(vmem_limit_bytes=16 * 2**20),
        name="layer_norm_backward",
    )(*parts, xhat, inverse, gain)


def conv_kernel(own, up, down, left, right, ul, ur, dl, dr, kernel, grad, out, pad):
    low, mid, high = slice(0, 3), slice(3, 11), slice(11, 14)
    west, here, east = slice(0, 3), slice(3, 19), slice(19, 22)
    for rows, cols, ref in (
        (mid, here, own),
        (low, here, up),
        (high, here, down),
        (mid, west, left),
        (mid, east, right),
        (low, west, ul),
        (low, east, ur),
        (high, west, dl),
        (high, east, dr),
    ):
        pad[rows, cols, :] = ref[...].astype(f32)
    total = None
    for col_tap in range(TAPS):
        column = pad[:, TAPS - 1 - col_tap : TAPS - 1 - col_tap + TILE_COLS, :]
        for row_tap in range(TAPS):
            start = TAPS - 1 - row_tap
            n = row_tap * TAPS + col_tap
            term = column[start : start + TILE_ROWS] * kernel[n : n + 1, :][None]
            total = term if total is None else total + term
    out[...] = (grad[...].astype(f32) + total).astype(bf16)


def convolution(own, halos, kernel, grad):
    width = 128

    def spec(shape):
        lead = (0,) * (len(shape) - 1)
        return pl.BlockSpec((*shape[:-1], width), lambda i: (*lead, i))

    operands = [own, *halos, kernel, grad]
    return pl.pallas_call(
        conv_kernel,
        grid=(CHAN // width,),
        out_shape=jax.ShapeDtypeStruct(grad.shape, bf16),
        in_specs=[spec(v.shape) for v in operands],
        out_specs=spec(grad.shape),
        scratch_shapes=[pltpu.VMEM((14, 24, width), f32)],
        compiler_params=pltpu.CompilerParams(vmem_limit_bytes=8 * 2**20),
        name="convolution",
    )(*operands)


def place(where, d, k, r):
    y, c = where[0], where[1]
    row = (k // 4 * 8 + lax.rem(y + r, NY) * 2 + lax.rem(c + d, 2)) * ROWS
    return pl.multiple_of(row, 32), slice(k % 4 * COLS, k % 4 * COLS + COLS)


def compute_kernel(where, *refs):
    n = 0

    def take(count):
        nonlocal n
        n += count
        return refs[n - count : n]

    bias = take(1)[0]
    tok = take(NX)
    first = take(2)
    second = [take(NY), take(NY)]
    out_y = take(2)
    out_z = take(2)
    gn = take(NX)
    w, xs, xt, acts, g = take(5)
    for i in range(NX):
        rows = slice(i * BLOCK, (i + 1) * BLOCK)
        xs[0, rows, :] = tok[i][:BLOCK]
        xs[1, rows, :] = tok[i][BLOCK:]
    for d in range(2):
        for k in range(NZ):
            for r in range(NY):
                row, col = place(where, d, k, r)
                for m in range(2):
                    row2 = pl.multiple_of(row + AY, 32)
                    w[m, pl.ds(row, AY), col] = first[d][k, r, m]
                    w[m, pl.ds(row2, BY), col] = second[d][r][k, m]
    for m in range(2):
        for i in range(CHAN // 256):
            xt[m, i * 256 : (i + 1) * 256, :] = xs[m, :, i * 256 : (i + 1) * 256].T

    width = 256

    def activations(i, _):
        cols = pl.ds(pl.multiple_of(i * width, width), width)
        pre = jnp.dot(xs[0], w[0, :, cols], preferred_element_type=f32) + bias[:, cols]
        back = jnp.dot(xs[1], w[1, :, cols], preferred_element_type=f32)
        cdf = 0.5 * (1.0 + lax.erf(pre * root_half))
        slope = cdf + pre * jnp.exp(-0.5 * pre * pre) * density_norm
        act = (pre * cdf).astype(bf16)
        acts[:, cols] = (back * slope).astype(bf16)
        g[:, cols] = jnp.dot(xt[1], act, preferred_element_type=f32).astype(bf16)
        return 0

    def flush(m):
        for d in range(2):
            for k in range(NZ):
                for r in range(NY):
                    row, col = place(where, d, k, r)
                    row2 = pl.multiple_of(row + AY, 32)
                    out_z[d][k, r, m] = g[pl.ds(row, AY), col]
                    out_y[d][r, k, m] = g[pl.ds(row2, BY), col]

    lax.fori_loop(0, HIDDEN // width, activations, 0)
    flush(1)

    def gradient_in(i, _):
        cols = pl.ds(pl.multiple_of(i * width, width), width)
        g[:, cols] = jnp.dot(xt[0], acts[:, cols], preferred_element_type=f32).astype(bf16)
        return 0

    lax.fori_loop(0, HIDDEN // width, gradient_in, 0)
    flush(0)

    def gradient_normed(i, _):
        cols = pl.ds(pl.multiple_of(i * width, width), width)
        part = lax.dot_general(
            acts[...], w[0, cols, :], (((1,), (1,)), ((), ())), preferred_element_type=f32
        ).astype(bf16)
        for b in range(NX):
            gn[b][:, cols] = part[b * BLOCK : (b + 1) * BLOCK]
        return 0

    lax.fori_loop(0, CHAN // width, gradient_normed, 0)


def compute(where, bias, tok, first, second):
    vmem = pl.BlockSpec(memory_space=pltpu.VMEM)
    gy = jax.ShapeDtypeStruct((NY, NZ, 2, BY, COLS), bf16)
    gz = jax.ShapeDtypeStruct((NZ, NY, 2, AY, COLS), bf16)
    gn = jax.ShapeDtypeStruct((BLOCK, CHAN), bf16)
    operands = [bias, *tok, *first, *second[0], *second[1]]
    out = pl.pallas_call(
        compute_kernel,
        out_shape=[gy, gy, gz, gz] + [gn] * NX,
        in_specs=[pl.BlockSpec(memory_space=pltpu.SMEM)] + [vmem] * len(operands),
        out_specs=[vmem] * (4 + NX),
        scratch_shapes=[
            pltpu.VMEM((2, CHAN, HIDDEN), bf16),
            pltpu.VMEM((2, TOKENS, CHAN), bf16),
            pltpu.VMEM((2, CHAN, TOKENS), bf16),
            pltpu.VMEM((TOKENS, HIDDEN), bf16),
            pltpu.VMEM((CHAN, HIDDEN), bf16),
        ],
        compiler_params=pltpu.CompilerParams(vmem_limit_bytes=60 * 2**20),
        cost_estimate=pl.CostEstimate(
            flops=10 * TOKENS * CHAN * HIDDEN, bytes_accessed=25_000_000, transcendentals=0
        ),
        name="block",
    )(where, *operands)
    return out[0:2], out[2:4], out[4:]


def add_kernel(*refs):
    own_y, got_y, own_z, got_z = refs[:4]
    ys, zs = refs[4 : 4 + NY], refs[4 + NY]
    for r in range(NY):
        for k in range(NZ):
            ys[r][k] = (own_y[r, k].astype(f32) + got_y[r, k].astype(f32)).astype(bf16)
    for k in range(NZ):
        for r in range(NY):
            zs[k, r] = (own_z[k, r].astype(f32) + got_z[k, r].astype(f32)).astype(bf16)


def add_cores(own_y, got_y, own_z, got_z):
    vmem = pl.BlockSpec(memory_space=pltpu.VMEM)
    out = pl.pallas_call(
        add_kernel,
        out_shape=[jax.ShapeDtypeStruct(own_y.shape[1:], bf16)] * NY
        + [jax.ShapeDtypeStruct(own_z.shape, bf16)],
        in_specs=[vmem] * 4,
        out_specs=[vmem] * (NY + 1),
        compiler_params=pltpu.CompilerParams(vmem_limit_bytes=40 * 2**20),
        name="add_cores",
    )(own_y, got_y, own_z, got_z)
    return out[:NY], out[NY]


def sum_y_kernel(*refs):
    for k in range(NZ):
        total = refs[0][k].astype(f32)
        for ref in refs[1:NY]:
            total = total + ref[k].astype(f32)
        refs[NY][k] = total.astype(bf16)


def sum_y(parts):
    vmem = pl.BlockSpec(memory_space=pltpu.VMEM)
    return pl.pallas_call(
        sum_y_kernel,
        out_shape=jax.ShapeDtypeStruct(parts[0].shape, bf16),
        in_specs=[vmem] * NY,
        out_specs=vmem,
        compiler_params=pltpu.CompilerParams(vmem_limit_bytes=24 * 2**20),
        name="sum_y",
    )(*parts)


def sum_z_kernel(parts, *outs):
    for r in range(NY):
        total = parts[0, r].astype(f32)
        for k in range(1, NZ):
            total = total + parts[k, r].astype(f32)
        outs[r][...] = total.astype(bf16)


def sum_z(parts):
    vmem = pl.BlockSpec(memory_space=pltpu.VMEM)
    return pl.pallas_call(
        sum_z_kernel,
        out_shape=[jax.ShapeDtypeStruct(parts.shape[2:], bf16)] * NY,
        in_specs=[vmem],
        out_specs=[vmem] * NY,
        compiler_params=pltpu.CompilerParams(vmem_limit_bytes=24 * 2**20),
        name="sum_z",
    )(parts)


def total(parts):
    result = parts[0].astype(f32)
    for part in parts[1:]:
        result = result + part.astype(f32)
    return result


def body(
    conv_out, out_grad, layer_norm_gain, layer_norm_bias, w_in, b_in, w_out, layer_scale, dw_kernel
):
    gain, shift_row, scale = (
        v.reshape(1, CHAN) for v in (layer_norm_gain, layer_norm_bias, layer_scale)
    )
    token, xhat, inverse = layer_norm(
        conv_out.reshape(BLOCK, CHAN), out_grad.reshape(BLOCK, CHAN), gain, shift_row, scale
    )
    tok = [to_x(token, -r) for r in range(NX)]

    shards = jnp.stack([w_in, w_out.T])
    lead, rest = shards[:, :AY], shards[:, AY:]
    got = gather_z(jnp.concatenate([rest.reshape(2 * BY, COLS), bias_rows(b_in)]))
    lead_y = jnp.stack([to_y(lead, -r) for r in range(NY)])
    got, lead_y, tok[1], tok[3] = lax.optimization_barrier((got, lead_y, tok[1], tok[3]))
    rest_z = got[:, : 2 * BY].reshape(NZ, 2, BY, COLS)
    bias = jnp.sum(got[:4, 2 * BY : 2 * BY + 3].astype(f32), axis=1).reshape(1, HIDDEN)
    second = [to_y(rest_z, -r) for r in range(NY)]
    first = gather_z(lead_y)
    second = [second, [swap(v) for v in second]]
    first = [first, swap(first)]

    where = jnp.stack([lax.axis_index("y"), lax.axis_index("c")]).astype(jnp.int32)
    grad_y, grad_z, part = compute(where, bias, tok, first, second)

    part = [to_x(v, r) for r, v in enumerate(part)]
    other_y, other_z, part[1], part[3] = lax.optimization_barrier(
        (swap(grad_y[1]), swap(grad_z[1]), part[1], part[3])
    )
    ys, zs = add_cores(grad_y[0], other_y, grad_z[0], other_z)
    ys = [to_y(v, r) for r, v in enumerate(ys)]
    own, *halos = layer_norm_backward(part, xhat, inverse, gain)
    halos = [to_tile(v, *where[:2]) for v, where in zip(halos, HALO, strict=True)]
    ys = sum_y(ys)
    ys, own, *halos = lax.optimization_barrier((ys, own, *halos))
    zs = sum_z(exchange_z(zs))
    own, *zs = lax.optimization_barrier((own, *zs))
    zs = [to_y(v, r) for r, v in enumerate(zs)]
    ys = exchange_z(ys)
    grad_input = convolution(own, halos, dw_kernel.reshape(TAPS * TAPS, CHAN), out_grad)
    grad_input, ys = lax.optimization_barrier((grad_input, ys))
    factor = 1.0 / math.sqrt(BLOCK * lax.axis_size(FINE))
    summed = jnp.concatenate([total(zs), total(ys)], axis=1) * factor
    return (grad_input, summed[0], summed[1].T)


def solution(mesh):
    fine = Mesh(mesh.devices.reshape(SIZES), FINE)
    token = P(STRIP, TENSOR, None)
    return jax.shard_map(
        body,
        mesh=fine,
        in_specs=(
            token,
            token,
            P(),
            P(),
            P(STRIP, TENSOR),
            P(TENSOR),
            P(TENSOR, STRIP),
            P(),
            P(),
        ),
        out_specs=(token, P(STRIP, TENSOR), P(TENSOR, STRIP)),
        check_vma=False,
    )
```

```python
import math

import jax
import jax.numpy as jnp
from jax import lax
from jax.experimental import pallas as pl
from jax.experimental.pallas import tpu as pltpu
from jax.sharding import Mesh
from jax.sharding import PartitionSpec as P

ln_eps = 1e-06
root_half = 0.7071067811865476
density_norm = 0.3989422804014327

FINE = ("zl", "y", "c", "x", "zh")
SIZES = (2, 4, 2, 4, 4)
STRIP = ("zl", "y", "c")
TENSOR = ("x", "zh")
Z = ("zl", "zh")
NX, NY, NZ = 4, 4, 8
CHAN, HIDDEN = 1536, 1536
ROWS, COLS = 96, 384
AY, BY = 32, 64
BLOCK = 128
TOKENS = BLOCK * NX

bf16, f32 = jnp.bfloat16, jnp.float32


def shift(n, k):
    return [(i, (i + k) % n) for i in range(n)]


def to_x(value, k):
    return lax.ppermute(value, "x", shift(NX, k)) if k else value


def to_y(value, k):
    return lax.ppermute(value, "y", shift(NY, k)) if k else value


def exchange_z(value):
    return lax.all_to_all(value, Z, 0, 0, tiled=True)


def bias_rows(bias):
    rows = []
    for _ in range(3):
        term = lax.reduce_precision(bias, 8, 7)
        rows.append(term.astype(bf16))
        bias = bias - term
    return jnp.concatenate([jnp.stack(rows), jnp.zeros((13, COLS), bf16)])


def gather_z(value):
    return exchange_z(jnp.broadcast_to(value, (NZ, *value.shape)))


def swap(value):
    return lax.ppermute(value, "c", shift(2, 1))


TILE_ROWS, TILE_COLS, TAPS, MARGIN = 8, 16, 7, 3


def to_tile(value, down, right):
    pairs = [
        (s * 16 + t, (s + down) * 16 + t + right)
        for s in range(16)
        for t in range(16)
        if 0 <= s + down < 16 and 0 <= t + right < 16
    ]
    return lax.ppermute(value, FINE, pairs)


def vmem_specs(count):
    return [pl.BlockSpec(memory_space=pltpu.VMEM)] * count


def norm_kernel(x, grad, gain, bias, scale, token, xhat, inverse):
    for i in range(0, BLOCK, 16):
        rows = slice(i, i + 16)
        value = x[rows].astype(f32)
        value = value - jnp.mean(value, axis=-1, keepdims=True)
        inv = lax.rsqrt(jnp.mean(value * value, axis=-1, keepdims=True) + ln_eps)
        value = value * inv
        xhat[rows] = value
        inverse[rows] = inv
        token[rows] = (value * gain[...] + bias[...]).astype(bf16)
        token[i + BLOCK : i + BLOCK + 16] = (grad[rows].astype(f32) * scale[...]).astype(bf16)


def layer_norm(x, grad, gain, bias, scale):
    return pl.pallas_call(
        norm_kernel,
        out_shape=[
            jax.ShapeDtypeStruct((2 * BLOCK, CHAN), bf16),
            jax.ShapeDtypeStruct((BLOCK, CHAN), f32),
            jax.ShapeDtypeStruct((BLOCK, 1), f32),
        ],
        in_specs=vmem_specs(5),
        out_specs=vmem_specs(3),
        compiler_params=pltpu.CompilerParams(vmem_limit_bytes=16 * 2**20),
        name="layer_norm",
    )(x, grad, gain, bias, scale)


def norm_backward_kernel(*refs):
    parts, (xhat, inverse, gain, out, first_cols, last_cols) = refs[:NX], refs[NX:]
    for i in range(TILE_ROWS):
        rows = slice(i * TILE_COLS, (i + 1) * TILE_COLS)
        value = parts[0][rows].astype(f32)
        for part in parts[1:]:
            value = value + part[rows].astype(f32)
        value = value * gain[...]
        hat = xhat[rows]
        first = jnp.mean(value, axis=-1, keepdims=True)
        second = jnp.mean(value * hat, axis=-1, keepdims=True)
        value = inverse[rows] * (value - first - hat * second)
        out[i] = value.astype(bf16)
        first_cols[i] = value[:MARGIN].astype(bf16)
        last_cols[i] = value[TILE_COLS - MARGIN :].astype(bf16)


def layer_norm_backward(parts, xhat, inverse, gain):
    return pl.pallas_call(
        norm_backward_kernel,
        out_shape=[jax.ShapeDtypeStruct((TILE_ROWS, TILE_COLS, CHAN), bf16)]
        + [jax.ShapeDtypeStruct((TILE_ROWS, MARGIN, CHAN), bf16)] * 2,
        in_specs=vmem_specs(NX + 3),
        out_specs=vmem_specs(3),
        compiler_params=pltpu.CompilerParams(vmem_limit_bytes=16 * 2**20),
        name="layer_norm_backward",
    )(*parts, xhat, inverse, gain)


def widen(out, rows, own, left, right):
    out[:, :MARGIN] = left[rows].astype(out.dtype)
    out[:, MARGIN : MARGIN + TILE_COLS] = own[rows].astype(out.dtype)
    out[:, MARGIN + TILE_COLS : TILE_COLS + 2 * MARGIN] = right[rows].astype(out.dtype)


def edge_kernel(own, left, right, first_rows, last_rows, scratch):
    for out, rows in ((first_rows, slice(0, 3)), (last_rows, slice(5, 8))):
        scratch[:, 16:, :] = jnp.zeros((MARGIN, 8, CHAN), f32)
        widen(scratch, rows, own, left, right)
        out[...] = scratch[...].astype(bf16)


def edges(own, left, right):
    return pl.pallas_call(
        edge_kernel,
        out_shape=[jax.ShapeDtypeStruct((MARGIN, 24, CHAN), bf16)] * 2,
        in_specs=vmem_specs(3),
        out_specs=vmem_specs(2),
        scratch_shapes=[pltpu.VMEM((MARGIN, 24, CHAN), f32)],
        compiler_params=pltpu.CompilerParams(vmem_limit_bytes=8 * 2**20),
        name="edges",
    )(own, left, right)


def conv_kernel(own, left, right, up, down, kernel, grad, out, pad):
    pad[:MARGIN] = up[...].astype(f32)
    widen(pad.at[MARGIN : MARGIN + TILE_ROWS], slice(0, TILE_ROWS), own, left, right)
    pad[MARGIN + TILE_ROWS :] = down[...].astype(f32)
    total = None
    for col_tap in range(TAPS):
        column = pad[:, TAPS - 1 - col_tap : TAPS - 1 - col_tap + TILE_COLS, :]
        for row_tap in range(TAPS):
            start = TAPS - 1 - row_tap
            n = row_tap * TAPS + col_tap
            term = column[start : start + TILE_ROWS] * kernel[n : n + 1, :][None]
            total = term if total is None else total + term
    out[...] = (grad[...].astype(f32) + total).astype(bf16)


def convolution(own, left, right, up, down, kernel, grad):
    width = 128

    def spec(shape):
        lead = (0,) * (len(shape) - 1)
        return pl.BlockSpec((*shape[:-1], width), lambda i: (*lead, i))

    operands = [own, left, right, up, down, kernel, grad]
    return pl.pallas_call(
        conv_kernel,
        grid=(CHAN // width,),
        out_shape=jax.ShapeDtypeStruct(grad.shape, bf16),
        in_specs=[spec(v.shape) for v in operands],
        out_specs=spec(grad.shape),
        scratch_shapes=[pltpu.VMEM((14, 24, width), f32)],
        compiler_params=pltpu.CompilerParams(vmem_limit_bytes=8 * 2**20),
        name="convolution",
    )(*operands)


def place(where, d, k, r):
    y, c = where[0], where[1]
    row = (k // 4 * 8 + lax.rem(y + r, NY) * 2 + lax.rem(c + d, 2)) * ROWS
    return pl.multiple_of(row, 32), slice(k % 4 * COLS, k % 4 * COLS + COLS)


def compute_kernel(where, *refs):
    n = 0

    def take(count):
        nonlocal n
        n += count
        return refs[n - count : n]

    bias = take(1)[0]
    tok = take(NX)
    first = take(2)
    second = [take(NY), take(NY)]
    out_y = take(2)
    out_z = take(2)
    gn = take(NX)
    w, xs, xt, acts, g = take(5)
    for i in range(NX):
        rows = slice(i * BLOCK, (i + 1) * BLOCK)
        xs[0, rows, :] = tok[i][:BLOCK]
        xs[1, rows, :] = tok[i][BLOCK:]
    for d in range(2):
        for k in range(NZ):
            for r in range(NY):
                row, col = place(where, d, k, r)
                for m in range(2):
                    row2 = pl.multiple_of(row + AY, 32)
                    w[m, pl.ds(row, AY), col] = first[d][k, r, m]
                    w[m, pl.ds(row2, BY), col] = second[d][r][k, m]
    for m in range(2):
        for i in range(CHAN // 256):
            xt[m, i * 256 : (i + 1) * 256, :] = xs[m, :, i * 256 : (i + 1) * 256].T

    width = 256

    def activations(i, _):
        cols = pl.ds(pl.multiple_of(i * width, width), width)
        pre = jnp.dot(xs[0], w[0, :, cols], preferred_element_type=f32) + bias[:, cols]
        back = jnp.dot(xs[1], w[1, :, cols], preferred_element_type=f32)
        cdf = 0.5 * (1.0 + lax.erf(pre * root_half))
        slope = cdf + pre * jnp.exp(-0.5 * pre * pre) * density_norm
        act = (pre * cdf).astype(bf16)
        acts[:, cols] = (back * slope).astype(bf16)
        g[:, cols] = jnp.dot(xt[1], act, preferred_element_type=f32).astype(bf16)
        return 0

    def flush(m):
        for d in range(2):
            for k in range(NZ):
                for r in range(NY):
                    row, col = place(where, d, k, r)
                    row2 = pl.multiple_of(row + AY, 32)
                    out_z[d][k, r, m] = g[pl.ds(row, AY), col]
                    out_y[d][r, k, m] = g[pl.ds(row2, BY), col]

    lax.fori_loop(0, HIDDEN // width, activations, 0)
    flush(1)

    def gradient_in(i, _):
        cols = pl.ds(pl.multiple_of(i * width, width), width)
        g[:, cols] = jnp.dot(xt[0], acts[:, cols], preferred_element_type=f32).astype(bf16)
        return 0

    lax.fori_loop(0, HIDDEN // width, gradient_in, 0)
    flush(0)

    def gradient_normed(i, _):
        cols = pl.ds(pl.multiple_of(i * width, width), width)
        part = lax.dot_general(
            acts[...], w[0, cols, :], (((1,), (1,)), ((), ())), preferred_element_type=f32
        ).astype(bf16)
        for b in range(NX):
            gn[b][:, cols] = part[b * BLOCK : (b + 1) * BLOCK]
        return 0

    lax.fori_loop(0, CHAN // width, gradient_normed, 0)


def compute(where, bias, tok, first, second):
    vmem = pl.BlockSpec(memory_space=pltpu.VMEM)
    gy = jax.ShapeDtypeStruct((NY, NZ, 2, BY, COLS), bf16)
    gz = jax.ShapeDtypeStruct((NZ, NY, 2, AY, COLS), bf16)
    gn = jax.ShapeDtypeStruct((BLOCK, CHAN), bf16)
    operands = [bias, *tok, *first, *second[0], *second[1]]
    out = pl.pallas_call(
        compute_kernel,
        out_shape=[gy, gy, gz, gz] + [gn] * NX,
        in_specs=[pl.BlockSpec(memory_space=pltpu.SMEM)] + [vmem] * len(operands),
        out_specs=[vmem] * (4 + NX),
        scratch_shapes=[
            pltpu.VMEM((2, CHAN, HIDDEN), bf16),
            pltpu.VMEM((2, TOKENS, CHAN), bf16),
            pltpu.VMEM((2, CHAN, TOKENS), bf16),
            pltpu.VMEM((TOKENS, HIDDEN), bf16),
            pltpu.VMEM((CHAN, HIDDEN), bf16),
        ],
        compiler_params=pltpu.CompilerParams(vmem_limit_bytes=60 * 2**20),
        cost_estimate=pl.CostEstimate(
            flops=10 * TOKENS * CHAN * HIDDEN, bytes_accessed=25_000_000, transcendentals=0
        ),
        name="block",
    )(where, *operands)
    return out[0:2], out[2:4], out[4:]


def add_kernel(*refs):
    own_y, got_y, own_z, got_z = refs[:4]
    ys, zs = refs[4 : 4 + NY], refs[4 + NY]
    for r in range(NY):
        for k in range(NZ):
            ys[r][k] = (own_y[r, k].astype(f32) + got_y[r, k].astype(f32)).astype(bf16)
    for k in range(NZ):
        for r in range(NY):
            zs[k, r] = (own_z[k, r].astype(f32) + got_z[k, r].astype(f32)).astype(bf16)


def add_cores(own_y, got_y, own_z, got_z):
    vmem = pl.BlockSpec(memory_space=pltpu.VMEM)
    out = pl.pallas_call(
        add_kernel,
        out_shape=[jax.ShapeDtypeStruct(own_y.shape[1:], bf16)] * NY
        + [jax.ShapeDtypeStruct(own_z.shape, bf16)],
        in_specs=[vmem] * 4,
        out_specs=[vmem] * (NY + 1),
        compiler_params=pltpu.CompilerParams(vmem_limit_bytes=40 * 2**20),
        name="add_cores",
    )(own_y, got_y, own_z, got_z)
    return out[:NY], out[NY]


def sum_y_kernel(*refs):
    for k in range(NZ):
        total = refs[0][k].astype(f32)
        for ref in refs[1:NY]:
            total = total + ref[k].astype(f32)
        refs[NY][k] = total.astype(bf16)


def sum_y(parts):
    vmem = pl.BlockSpec(memory_space=pltpu.VMEM)
    return pl.pallas_call(
        sum_y_kernel,
        out_shape=jax.ShapeDtypeStruct(parts[0].shape, bf16),
        in_specs=[vmem] * NY,
        out_specs=vmem,
        compiler_params=pltpu.CompilerParams(vmem_limit_bytes=24 * 2**20),
        name="sum_y",
    )(*parts)


def sum_z_kernel(parts, *outs):
    for r in range(NY):
        total = parts[0, r].astype(f32)
        for k in range(1, NZ):
            total = total + parts[k, r].astype(f32)
        outs[r][...] = total.astype(bf16)


def sum_z(parts):
    vmem = pl.BlockSpec(memory_space=pltpu.VMEM)
    return pl.pallas_call(
        sum_z_kernel,
        out_shape=[jax.ShapeDtypeStruct(parts.shape[2:], bf16)] * NY,
        in_specs=[vmem],
        out_specs=[vmem] * NY,
        compiler_params=pltpu.CompilerParams(vmem_limit_bytes=24 * 2**20),
        name="sum_z",
    )(parts)


def finish_kernel(*refs):
    zs, (ys, grad_in, grad_out) = refs[:NY], refs[NY:]
    factor = 1.0 / math.sqrt(BLOCK * 256)
    for m in range(2):
        lead = zs[0][m].astype(f32)
        for part in zs[1:]:
            lead = lead + part[m].astype(f32)
        rest = ys[0, m].astype(f32)
        for k in range(1, NZ):
            rest = rest + ys[k, m].astype(f32)
        value = jnp.concatenate([lead, rest]) * factor
        if m == 0:
            grad_in[...] = value
        else:
            grad_out[...] = value.T


def finish(zs, ys):
    return pl.pallas_call(
        finish_kernel,
        out_shape=[
            jax.ShapeDtypeStruct((ROWS, COLS), f32),
            jax.ShapeDtypeStruct((COLS, ROWS), f32),
        ],
        in_specs=vmem_specs(NY + 1),
        out_specs=vmem_specs(2),
        compiler_params=pltpu.CompilerParams(vmem_limit_bytes=8 * 2**20),
        name="finish",
    )(*zs, ys)


def body(
    conv_out, out_grad, layer_norm_gain, layer_norm_bias, w_in, b_in, w_out, layer_scale, dw_kernel
):
    gain, shift_row, scale = (
        v.reshape(1, CHAN) for v in (layer_norm_gain, layer_norm_bias, layer_scale)
    )
    token, xhat, inverse = layer_norm(
        conv_out.reshape(BLOCK, CHAN), out_grad.reshape(BLOCK, CHAN), gain, shift_row, scale
    )
    tok = [to_x(token, -r) for r in range(NX)]

    shards = jnp.stack([w_in, w_out.T])
    lead, rest = shards[:, :AY], shards[:, AY:]
    got = gather_z(jnp.concatenate([rest.reshape(2 * BY, COLS), bias_rows(b_in)]))
    lead_y = jnp.stack([to_y(lead, -r) for r in range(NY)])
    got, lead_y, tok[1], tok[3] = lax.optimization_barrier((got, lead_y, tok[1], tok[3]))
    rest_z = got[:, : 2 * BY].reshape(NZ, 2, BY, COLS)
    bias = jnp.sum(got[:4, 2 * BY : 2 * BY + 3].astype(f32), axis=1).reshape(1, HIDDEN)
    second = [to_y(rest_z, -r) for r in range(NY)]
    first = gather_z(lead_y)
    swapped = [swap(v) for v in second[:2]] + [None, swap(second[3])]
    first, swapped[1], swapped[3], second[2], tok[2] = lax.optimization_barrier(
        (first, swapped[1], swapped[3], second[2], tok[2])
    )
    swapped[2] = swap(second[2])
    second = [second, swapped]
    first = [first, swap(first)]

    where = jnp.stack([lax.axis_index("y"), lax.axis_index("c")]).astype(jnp.int32)
    grad_y, grad_z, part = compute(where, bias, tok, first, second)

    part = [to_x(v, r) for r, v in enumerate(part)]
    other_y, other_z, part[1], part[3] = lax.optimization_barrier(
        (swap(grad_y[1]), swap(grad_z[1]), part[1], part[3])
    )
    ys, zs = add_cores(grad_y[0], other_y, grad_z[0], other_z)
    ys = [to_y(v, r) for r, v in enumerate(ys)]
    own, first_cols, last_cols = layer_norm_backward(part, xhat, inverse, gain)
    left, right = to_tile(last_cols, 0, 1), to_tile(first_cols, 0, -1)
    ys = sum_y(ys)
    ys, own, left, right = lax.optimization_barrier((ys, own, left, right))
    zs = sum_z(exchange_z(zs))
    left, right, *zs = lax.optimization_barrier((left, right, *zs))
    first_rows, last_rows = edges(own, left, right)
    up, down = to_tile(last_rows, 1, 0), to_tile(first_rows, -1, 0)
    zs = [to_y(v, r) for r, v in enumerate(zs)]
    ys = exchange_z(ys)
    kernel = dw_kernel.reshape(TAPS * TAPS, CHAN)
    grad_input = convolution(own, left, right, up, down, kernel, out_grad)
    grad_input, ys = lax.optimization_barrier((grad_input, ys))
    grad_in, grad_out = finish(zs, ys)
    return (grad_input, grad_in, grad_out)


def solution(mesh):
    fine = Mesh(mesh.devices.reshape(SIZES), FINE)
    token = P(STRIP, TENSOR, None)
    return jax.shard_map(
        body,
        mesh=fine,
        in_specs=(
            token,
            token,
            P(),
            P(),
            P(STRIP, TENSOR),
            P(TENSOR),
            P(TENSOR, STRIP),
            P(),
            P(),
        ),
        out_specs=(token, P(STRIP, TENSOR), P(TENSOR, STRIP)),
        check_vma=False,
    )
```

```python
import math

import jax
import jax.numpy as jnp
from jax import lax
from jax.experimental import pallas as pl
from jax.experimental.pallas import tpu as pltpu
from jax.sharding import Mesh
from jax.sharding import PartitionSpec as P

ln_eps = 1e-06
root_half = 0.7071067811865476
density_norm = 0.3989422804014327

FINE = ("zl", "y", "c", "x", "zh")
SIZES = (2, 4, 2, 4, 4)
STRIP = ("zl", "y", "c")
TENSOR = ("x", "zh")
Z = ("zl", "zh")
NX, NY, NZ = 4, 4, 8
CHAN, HIDDEN = 1536, 1536
ROWS, COLS = 96, 384
PLANES = 8
AY, BY = 32, 64
BLOCK = 128
TOKENS = BLOCK * NX

bf16, f32 = jnp.bfloat16, jnp.float32


def shift(n, k):
    return [(i, (i + k) % n) for i in range(n)]


def to_x(value, k):
    return lax.ppermute(value, "x", shift(NX, k)) if k else value


def to_y(value, k):
    return lax.ppermute(value, "y", shift(NY, k)) if k else value


def exchange_z(value):
    return lax.all_to_all(value, Z, 0, 0, tiled=True)


def bias_rows(bias):
    rows = []
    for _ in range(3):
        term = lax.reduce_precision(bias, 8, 7)
        rows.append(term.astype(bf16))
        bias = bias - term
    return jnp.concatenate([jnp.stack(rows), jnp.zeros((13, COLS), bf16)])


def gather_z(value):
    return exchange_z(jnp.broadcast_to(value, (NZ, *value.shape)))


def swap(value):
    return lax.ppermute(value, "c", shift(2, 1))


TILE_ROWS, TILE_COLS, TAPS, MARGIN = 8, 16, 7, 3


def to_tile(value, down, right):
    pairs = [
        (s * 16 + t, (s + down) * 16 + t + right)
        for s in range(16)
        for t in range(16)
        if 0 <= s + down < 16 and 0 <= t + right < 16
    ]
    return lax.ppermute(value, FINE, pairs)


def vmem_specs(count):
    return [pl.BlockSpec(memory_space=pltpu.VMEM)] * count


def norm_kernel(x, grad, gain, bias, scale, token, xhat, inverse):
    for i in range(0, BLOCK, 16):
        rows = slice(i, i + 16)
        value = x[rows].astype(f32)
        value = value - jnp.mean(value, axis=-1, keepdims=True)
        inv = lax.rsqrt(jnp.mean(value * value, axis=-1, keepdims=True) + ln_eps)
        value = value * inv
        xhat[rows] = value
        inverse[rows] = inv
        token[rows] = (value * gain[...] + bias[...]).astype(bf16)
        token[i + BLOCK : i + BLOCK + 16] = (grad[rows].astype(f32) * scale[...]).astype(bf16)


def layer_norm(x, grad, gain, bias, scale):
    return pl.pallas_call(
        norm_kernel,
        out_shape=[
            jax.ShapeDtypeStruct((2 * BLOCK, CHAN), bf16),
            jax.ShapeDtypeStruct((BLOCK, CHAN), f32),
            jax.ShapeDtypeStruct((BLOCK, 1), f32),
        ],
        in_specs=vmem_specs(5),
        out_specs=vmem_specs(3),
        compiler_params=pltpu.CompilerParams(vmem_limit_bytes=16 * 2**20),
        name="layer_norm",
    )(x, grad, gain, bias, scale)


def norm_backward_kernel(*refs):
    parts, (xhat, inverse, gain, out, first_cols, last_cols) = refs[:NX], refs[NX:]
    for i in range(TILE_ROWS):
        rows = slice(i * TILE_COLS, (i + 1) * TILE_COLS)
        value = parts[0][rows].astype(f32)
        for part in parts[1:]:
            value = value + part[rows].astype(f32)
        value = value * gain[...]
        hat = xhat[rows]
        first = jnp.mean(value, axis=-1, keepdims=True)
        second = jnp.mean(value * hat, axis=-1, keepdims=True)
        value = inverse[rows] * (value - first - hat * second)
        out[i] = value.astype(bf16)
        first_cols[i] = value[:MARGIN].astype(bf16)
        last_cols[i] = value[TILE_COLS - MARGIN :].astype(bf16)


def layer_norm_backward(parts, xhat, inverse, gain):
    return pl.pallas_call(
        norm_backward_kernel,
        out_shape=[jax.ShapeDtypeStruct((TILE_ROWS, TILE_COLS, CHAN), bf16)]
        + [jax.ShapeDtypeStruct((TILE_ROWS, MARGIN, CHAN), bf16)] * 2,
        in_specs=vmem_specs(NX + 3),
        out_specs=vmem_specs(3),
        compiler_params=pltpu.CompilerParams(vmem_limit_bytes=16 * 2**20),
        name="layer_norm_backward",
    )(*parts, xhat, inverse, gain)


def widen(out, rows, own, left, right):
    out[:, :MARGIN] = left[rows].astype(out.dtype)
    out[:, MARGIN : MARGIN + TILE_COLS] = own[rows].astype(out.dtype)
    out[:, MARGIN + TILE_COLS : TILE_COLS + 2 * MARGIN] = right[rows].astype(out.dtype)


def edge_kernel(own, left, right, first_rows, last_rows, scratch):
    for out, rows in ((first_rows, slice(0, 3)), (last_rows, slice(5, 8))):
        scratch[:, 16:, :] = jnp.zeros((MARGIN, 8, CHAN), f32)
        widen(scratch, rows, own, left, right)
        out[...] = scratch[...].astype(bf16)


def edges(own, left, right):
    return pl.pallas_call(
        edge_kernel,
        out_shape=[jax.ShapeDtypeStruct((MARGIN, 24, CHAN), bf16)] * 2,
        in_specs=vmem_specs(3),
        out_specs=vmem_specs(2),
        scratch_shapes=[pltpu.VMEM((MARGIN, 24, CHAN), f32)],
        compiler_params=pltpu.CompilerParams(vmem_limit_bytes=8 * 2**20),
        name="edges",
    )(own, left, right)


def conv_kernel(own, left, right, up, down, kernel, grad, out, pad):
    pad[:MARGIN] = up[...].astype(f32)
    widen(pad.at[MARGIN : MARGIN + TILE_ROWS], slice(0, TILE_ROWS), own, left, right)
    pad[MARGIN + TILE_ROWS :] = down[...].astype(f32)
    total = None
    for col_tap in range(TAPS):
        column = pad[:, TAPS - 1 - col_tap : TAPS - 1 - col_tap + TILE_COLS, :]
        for row_tap in range(TAPS):
            start = TAPS - 1 - row_tap
            n = row_tap * TAPS + col_tap
            term = column[start : start + TILE_ROWS] * kernel[n : n + 1, :][None]
            total = term if total is None else total + term
    out[...] = (grad[...].astype(f32) + total).astype(bf16)


def convolution(own, left, right, up, down, kernel, grad):
    width = 128

    def spec(shape):
        lead = (0,) * (len(shape) - 1)
        return pl.BlockSpec((*shape[:-1], width), lambda i: (*lead, i))

    operands = [own, left, right, up, down, kernel, grad]
    return pl.pallas_call(
        conv_kernel,
        grid=(CHAN // width,),
        out_shape=jax.ShapeDtypeStruct(grad.shape, bf16),
        in_specs=[spec(v.shape) for v in operands],
        out_specs=spec(grad.shape),
        scratch_shapes=[pltpu.VMEM((14, 24, width), f32)],
        compiler_params=pltpu.CompilerParams(vmem_limit_bytes=8 * 2**20),
        name="convolution",
    )(*operands)


def place(where, d, k, r):
    y, c = where[0], where[1]
    row = (k // 4 * 8 + lax.rem(y + r, NY) * 2 + lax.rem(c + d, 2)) * ROWS
    return pl.multiple_of(row, 32), slice(k % 4 * COLS, k % 4 * COLS + COLS)


def own_row(j, c):
    return pl.multiple_of((2 * j + c) * ROWS, 32)


def token_kernel(where, *refs):
    tok, (xs, mine, other, xt) = refs[:NX], refs[NX:]
    c = where[1]
    for i in range(NX):
        rows = slice(i * BLOCK, (i + 1) * BLOCK)
        xs[0, rows, :] = tok[i][:BLOCK]
        xs[1, rows, :] = tok[i][BLOCK:]
    for m in range(2):
        for i in range(CHAN // 256):
            xt[i * 256 : (i + 1) * 256, :] = xs[m, :, i * 256 : (i + 1) * 256].T
        for out, core in ((mine, c), (other, 1 - c)):
            for j in range(PLANES):
                row = own_row(j, core)
                row2 = pl.multiple_of(row + AY, 32)
                out[m, j * AY : (j + 1) * AY, :] = xt[pl.ds(row, AY), :]
                start = PLANES * AY + j * BY
                out[m, start : start + BY, :] = xt[pl.ds(row2, BY), :]


def tokens(where, tok):
    half = jax.ShapeDtypeStruct((2, CHAN // 2, TOKENS), bf16)
    return pl.pallas_call(
        token_kernel,
        out_shape=[jax.ShapeDtypeStruct((2, TOKENS, CHAN), bf16), half, half],
        in_specs=[pl.BlockSpec(memory_space=pltpu.SMEM)] + vmem_specs(NX),
        out_specs=vmem_specs(3),
        scratch_shapes=[pltpu.VMEM((CHAN, TOKENS), bf16)],
        compiler_params=pltpu.CompilerParams(vmem_limit_bytes=20 * 2**20),
        cost_estimate=pl.CostEstimate(flops=0, bytes_accessed=12_000_000, transcendentals=0),
        name="tokens",
    )(where, *tok)


def activation_kernel(where, *refs):
    bias, xs = refs[:2]
    first = refs[2:4]
    second = refs[4 : 4 + NY], refs[4 + NY : 4 + 2 * NY]
    act, pre_grad, w_in, w_out = refs[4 + 2 * NY :]
    for d in range(2):
        for k in range(NZ):
            for r in range(NY):
                row, col = place(where, d, k, r)
                row2 = pl.multiple_of(row + AY, 32)
                for m, w in ((0, w_in), (1, w_out)):
                    w[pl.ds(row, AY), col] = first[d][k, r, m]
                    w[pl.ds(row2, BY), col] = second[d][r][k, m]

    width = 256

    def step(i, _):
        cols = pl.ds(pl.multiple_of(i * width, width), width)
        pre = jnp.dot(xs[0], w_in[:, cols], preferred_element_type=f32) + bias[:, cols]
        back = jnp.dot(xs[1], w_out[:, cols], preferred_element_type=f32)
        cdf = 0.5 * (1.0 + lax.erf(pre * root_half))
        slope = cdf + pre * jnp.exp(-0.5 * pre * pre) * density_norm
        act[:, cols] = (pre * cdf).astype(bf16)
        pre_grad[:, cols] = (back * slope).astype(bf16)
        return 0

    lax.fori_loop(0, HIDDEN // width, step, 0)


def activations(where, bias, xs, first, second):
    operands = [bias, xs, *first, *second[0], *second[1]]
    out = jax.ShapeDtypeStruct((TOKENS, HIDDEN), bf16)
    return pl.pallas_call(
        activation_kernel,
        out_shape=[out, out, jax.ShapeDtypeStruct((CHAN, HIDDEN), bf16)],
        in_specs=[pl.BlockSpec(memory_space=pltpu.SMEM)] + vmem_specs(len(operands)),
        out_specs=vmem_specs(3),
        scratch_shapes=[pltpu.VMEM((CHAN, HIDDEN), bf16)],
        compiler_params=pltpu.CompilerParams(vmem_limit_bytes=40 * 2**20),
        cost_estimate=pl.CostEstimate(
            flops=4 * TOKENS * CHAN * HIDDEN, bytes_accessed=25_000_000, transcendentals=0
        ),
        name="activations",
    )(where, *operands)


def normed_kernel(pre_grad, w_in, *outs):
    width = 256

    def step(i, _):
        cols = pl.ds(pl.multiple_of(i * width, width), width)
        part = lax.dot_general(
            pre_grad[...], w_in[cols, :], (((1,), (1,)), ((), ())), preferred_element_type=f32
        ).astype(bf16)
        for b in range(NX):
            outs[b][:, cols] = part[b * BLOCK : (b + 1) * BLOCK]
        return 0

    lax.fori_loop(0, CHAN // width, step, 0)


def normed_gradient(pre_grad, w_in):
    return pl.pallas_call(
        normed_kernel,
        out_shape=[jax.ShapeDtypeStruct((BLOCK, CHAN), bf16)] * NX,
        in_specs=vmem_specs(2),
        out_specs=vmem_specs(NX),
        compiler_params=pltpu.CompilerParams(vmem_limit_bytes=20 * 2**20),
        cost_estimate=pl.CostEstimate(
            flops=2 * TOKENS * CHAN * HIDDEN, bytes_accessed=20_000_000, transcendentals=0
        ),
        name="normed_gradient",
    )(pre_grad, w_in)


def weight_kernel(where, mine, got, *refs):
    sides, (ys, out_z, g) = (refs[0:2], refs[2:4]), (refs[4 : 4 + NY], *refs[4 + NY :])
    width = 256
    for m in range(2):
        own, other = sides[m]

        def step(i, _, m=m, own=own, other=other):
            cols = pl.ds(pl.multiple_of(i * width, width), width)
            value = jnp.dot(mine[m], own[:, cols], preferred_element_type=f32)
            value = value + jnp.dot(got[m], other[:, cols], preferred_element_type=f32)
            g[:, cols] = value.astype(bf16)
            return 0

        lax.fori_loop(0, HIDDEN // width, step, 0)
        for k in range(NZ):
            col = slice(k % 4 * COLS, k % 4 * COLS + COLS)
            for r in range(NY):
                j = k // 4 * NY + lax.rem(where[0] + r, NY)
                row = pl.multiple_of(j * AY, 32)
                row2 = pl.multiple_of(PLANES * AY + j * BY, 32)
                out_z[k, r, m] = g[pl.ds(row, AY), col]
                ys[r][k, m] = g[pl.ds(row2, BY), col]


def weight_gradients(where, mine, got, pre_grad, other_pre_grad, act, other_act):
    operands = [mine, got, pre_grad, other_pre_grad, act, other_act]
    out = pl.pallas_call(
        weight_kernel,
        out_shape=[jax.ShapeDtypeStruct((NZ, 2, BY, COLS), bf16)] * NY
        + [jax.ShapeDtypeStruct((NZ, NY, 2, AY, COLS), bf16)],
        in_specs=[pl.BlockSpec(memory_space=pltpu.SMEM)] + vmem_specs(len(operands)),
        out_specs=vmem_specs(NY + 1),
        scratch_shapes=[pltpu.VMEM((CHAN // 2, HIDDEN), bf16)],
        compiler_params=pltpu.CompilerParams(vmem_limit_bytes=32 * 2**20),
        cost_estimate=pl.CostEstimate(
            flops=4 * TOKENS * CHAN * HIDDEN, bytes_accessed=30_000_000, transcendentals=0
        ),
        name="weight_gradients",
    )(where, *operands)
    return out[:NY], out[NY]


def sum_y_kernel(*refs):
    for k in range(NZ):
        total = refs[0][k].astype(f32)
        for ref in refs[1:NY]:
            total = total + ref[k].astype(f32)
        refs[NY][k] = total.astype(bf16)


def sum_y(parts):
    vmem = pl.BlockSpec(memory_space=pltpu.VMEM)
    return pl.pallas_call(
        sum_y_kernel,
        out_shape=jax.ShapeDtypeStruct(parts[0].shape, bf16),
        in_specs=[vmem] * NY,
        out_specs=vmem,
        compiler_params=pltpu.CompilerParams(vmem_limit_bytes=24 * 2**20),
        name="sum_y",
    )(*parts)


def sum_z_kernel(parts, *outs):
    for r in range(NY):
        total = parts[0, r].astype(f32)
        for k in range(1, NZ):
            total = total + parts[k, r].astype(f32)
        outs[r][...] = total.astype(bf16)


def sum_z(parts):
    vmem = pl.BlockSpec(memory_space=pltpu.VMEM)
    return pl.pallas_call(
        sum_z_kernel,
        out_shape=[jax.ShapeDtypeStruct(parts.shape[2:], bf16)] * NY,
        in_specs=[vmem],
        out_specs=[vmem] * NY,
        compiler_params=pltpu.CompilerParams(vmem_limit_bytes=24 * 2**20),
        name="sum_z",
    )(parts)


def finish_kernel(*refs):
    zs, (ys, grad_in, grad_out) = refs[:NY], refs[NY:]
    factor = 1.0 / math.sqrt(BLOCK * 256)
    for m in range(2):
        lead = zs[0][m].astype(f32)
        for part in zs[1:]:
            lead = lead + part[m].astype(f32)
        rest = ys[0, m].astype(f32)
        for k in range(1, NZ):
            rest = rest + ys[k, m].astype(f32)
        value = jnp.concatenate([lead, rest]) * factor
        if m == 0:
            grad_in[...] = value
        else:
            grad_out[...] = value.T


def finish(zs, ys):
    return pl.pallas_call(
        finish_kernel,
        out_shape=[
            jax.ShapeDtypeStruct((ROWS, COLS), f32),
            jax.ShapeDtypeStruct((COLS, ROWS), f32),
        ],
        in_specs=vmem_specs(NY + 1),
        out_specs=vmem_specs(2),
        compiler_params=pltpu.CompilerParams(vmem_limit_bytes=8 * 2**20),
        name="finish",
    )(*zs, ys)


def body(
    conv_out, out_grad, layer_norm_gain, layer_norm_bias, w_in, b_in, w_out, layer_scale, dw_kernel
):
    gain, shift_row, scale = (
        v.reshape(1, CHAN) for v in (layer_norm_gain, layer_norm_bias, layer_scale)
    )
    token, xhat, inverse = layer_norm(
        conv_out.reshape(BLOCK, CHAN), out_grad.reshape(BLOCK, CHAN), gain, shift_row, scale
    )
    tok = [to_x(token, -r) for r in range(NX)]

    shards = jnp.stack([w_in, w_out.T])
    lead, rest = shards[:, :AY], shards[:, AY:]
    got = gather_z(jnp.concatenate([rest.reshape(2 * BY, COLS), bias_rows(b_in)]))
    lead_y = jnp.stack([to_y(lead, -r) for r in range(NY)])
    got, lead_y, tok[1], tok[3] = lax.optimization_barrier((got, lead_y, tok[1], tok[3]))
    rest_z = got[:, : 2 * BY].reshape(NZ, 2, BY, COLS)
    bias = jnp.sum(got[:4, 2 * BY : 2 * BY + 3].astype(f32), axis=1).reshape(1, HIDDEN)
    second = [to_y(rest_z, -r) for r in range(NY)]
    first = gather_z(lead_y)
    swapped = [swap(v) for v in second[:2]] + [None, swap(second[3])]
    where = jnp.stack([lax.axis_index("y"), lax.axis_index("c")]).astype(jnp.int32)
    tok[2], second[2] = lax.optimization_barrier((tok[2], second[2]))
    xs, mine, other = tokens(where, tok)
    first, swapped[1], swapped[3], xs = lax.optimization_barrier(
        (first, swapped[1], swapped[3], xs)
    )
    other = swap(other)
    swapped[2] = swap(second[2])
    second = [second, swapped]
    first = [first, swap(first)]

    act, pre_grad, w_all = activations(where, bias, xs, first, second)
    other_act, other_pre_grad = swap(act), swap(pre_grad)
    part = normed_gradient(pre_grad, w_all)
    other_act, other_pre_grad, *part = lax.optimization_barrier(
        (other_act, other_pre_grad, *part)
    )
    part = [to_x(v, r) for r, v in enumerate(part)]
    ys, zs = weight_gradients(where, mine, other, pre_grad, other_pre_grad, act, other_act)
    ys = [to_y(v, r) for r, v in enumerate(ys)]
    own, first_cols, last_cols = layer_norm_backward(part, xhat, inverse, gain)
    left, right = to_tile(last_cols, 0, 1), to_tile(first_cols, 0, -1)
    ys = sum_y(ys)
    ys, own, left, right = lax.optimization_barrier((ys, own, left, right))
    zs = sum_z(exchange_z(zs))
    left, right, *zs = lax.optimization_barrier((left, right, *zs))
    first_rows, last_rows = edges(own, left, right)
    up, down = to_tile(last_rows, 1, 0), to_tile(first_rows, -1, 0)
    zs = [to_y(v, r) for r, v in enumerate(zs)]
    ys = exchange_z(ys)
    kernel = dw_kernel.reshape(TAPS * TAPS, CHAN)
    grad_input = convolution(own, left, right, up, down, kernel, out_grad)
    grad_input, ys = lax.optimization_barrier((grad_input, ys))
    grad_in, grad_out = finish(zs, ys)
    return (grad_input, grad_in, grad_out)


def solution(mesh):
    fine = Mesh(mesh.devices.reshape(SIZES), FINE)
    token = P(STRIP, TENSOR, None)
    return jax.shard_map(
        body,
        mesh=fine,
        in_specs=(
            token,
            token,
            P(),
            P(),
            P(STRIP, TENSOR),
            P(TENSOR),
            P(TENSOR, STRIP),
            P(),
            P(),
        ),
        out_specs=(token, P(STRIP, TENSOR), P(TENSOR, STRIP)),
        check_vma=False,
    )
```

```python
import functools
import math

import jax
import jax.numpy as jnp
from jax import lax
from jax.experimental import pallas as pl
from jax.experimental.pallas import tpu as pltpu
from jax.sharding import Mesh
from jax.sharding import PartitionSpec as P

ln_eps = 1e-06
root_half = 0.7071067811865476
density_norm = 0.3989422804014327

FINE = ("zl", "y", "c", "x", "zh")
SIZES = (2, 4, 2, 4, 4)
STRIP = ("zl", "y", "c")
TENSOR = ("x", "zh")
Z = ("zl", "zh")
NX, NY, NZ = 4, 4, 8
CHAN, HIDDEN = 1536, 1536
ROWS, COLS = 96, 384
PLANES = 8
AY, BY = 32, 64
BLOCK = 128
TOKENS = BLOCK * NX

bf16, f32 = jnp.bfloat16, jnp.float32


def shift(n, k):
    return [(i, (i + k) % n) for i in range(n)]


def to_x(value, k):
    return lax.ppermute(value, "x", shift(NX, k)) if k else value


def to_y(value, k):
    return lax.ppermute(value, "y", shift(NY, k)) if k else value


def exchange_z(value):
    return lax.all_to_all(value, Z, 0, 0, tiled=True)


def bias_rows(bias):
    rows = []
    for _ in range(3):
        term = lax.reduce_precision(bias, 8, 7)
        rows.append(term.astype(bf16))
        bias = bias - term
    return jnp.concatenate([jnp.stack(rows), jnp.zeros((13, COLS), bf16)])


def gather_z(value):
    return exchange_z(jnp.broadcast_to(value, (NZ, *value.shape)))


def swap(value):
    return lax.ppermute(value, "c", shift(2, 1))


TILE_ROWS, TILE_COLS, TAPS, MARGIN = 8, 16, 7, 3


def to_tile(value, down, right):
    pairs = [
        (s * 16 + t, (s + down) * 16 + t + right)
        for s in range(16)
        for t in range(16)
        if 0 <= s + down < 16 and 0 <= t + right < 16
    ]
    return lax.ppermute(value, FINE, pairs)


def vmem_specs(count):
    return [pl.BlockSpec(memory_space=pltpu.VMEM)] * count


def norm_kernel(x, grad, gain, bias, scale, token, xhat, inverse):
    for i in range(0, BLOCK, 16):
        rows = slice(i, i + 16)
        value = x[rows].astype(f32)
        value = value - jnp.mean(value, axis=-1, keepdims=True)
        inv = lax.rsqrt(jnp.mean(value * value, axis=-1, keepdims=True) + ln_eps)
        value = value * inv
        xhat[rows] = value
        inverse[rows] = inv
        token[rows] = (value * gain[...] + bias[...]).astype(bf16)
        token[i + BLOCK : i + BLOCK + 16] = (grad[rows].astype(f32) * scale[...]).astype(bf16)


def layer_norm(x, grad, gain, bias, scale):
    return pl.pallas_call(
        norm_kernel,
        out_shape=[
            jax.ShapeDtypeStruct((2 * BLOCK, CHAN), bf16),
            jax.ShapeDtypeStruct((BLOCK, CHAN), f32),
            jax.ShapeDtypeStruct((BLOCK, 1), f32),
        ],
        in_specs=vmem_specs(5),
        out_specs=vmem_specs(3),
        compiler_params=pltpu.CompilerParams(vmem_limit_bytes=16 * 2**20),
        name="layer_norm",
    )(x, grad, gain, bias, scale)


def norm_backward_kernel(*refs):
    parts, (xhat, inverse, gain, out, first_cols, last_cols) = refs[:NX], refs[NX:]
    for i in range(TILE_ROWS):
        rows = slice(i * TILE_COLS, (i + 1) * TILE_COLS)
        value = parts[0][rows].astype(f32)
        for part in parts[1:]:
            value = value + part[rows].astype(f32)
        value = value * gain[...]
        hat = xhat[rows]
        first = jnp.mean(value, axis=-1, keepdims=True)
        second = jnp.mean(value * hat, axis=-1, keepdims=True)
        value = inverse[rows] * (value - first - hat * second)
        out[i] = value.astype(bf16)
        first_cols[i] = value[:MARGIN].astype(bf16)
        last_cols[i] = value[TILE_COLS - MARGIN :].astype(bf16)


def layer_norm_backward(parts, xhat, inverse, gain):
    return pl.pallas_call(
        norm_backward_kernel,
        out_shape=[jax.ShapeDtypeStruct((TILE_ROWS, TILE_COLS, CHAN), bf16)]
        + [jax.ShapeDtypeStruct((TILE_ROWS, MARGIN, CHAN), bf16)] * 2,
        in_specs=vmem_specs(NX + 3),
        out_specs=vmem_specs(3),
        compiler_params=pltpu.CompilerParams(vmem_limit_bytes=16 * 2**20),
        name="layer_norm_backward",
    )(*parts, xhat, inverse, gain)


def widen(out, rows, own, left, right):
    out[:, :MARGIN] = left[rows].astype(out.dtype)
    out[:, MARGIN : MARGIN + TILE_COLS] = own[rows].astype(out.dtype)
    out[:, MARGIN + TILE_COLS : TILE_COLS + 2 * MARGIN] = right[rows].astype(out.dtype)


def edge_kernel(own, left, right, first_rows, last_rows, scratch):
    for out, rows in ((first_rows, slice(0, 3)), (last_rows, slice(5, 8))):
        scratch[:, 16:, :] = jnp.zeros((MARGIN, 8, CHAN), f32)
        widen(scratch, rows, own, left, right)
        out[...] = scratch[...].astype(bf16)


def edges(own, left, right):
    return pl.pallas_call(
        edge_kernel,
        out_shape=[jax.ShapeDtypeStruct((MARGIN, 24, CHAN), bf16)] * 2,
        in_specs=vmem_specs(3),
        out_specs=vmem_specs(2),
        scratch_shapes=[pltpu.VMEM((MARGIN, 24, CHAN), f32)],
        compiler_params=pltpu.CompilerParams(vmem_limit_bytes=8 * 2**20),
        name="edges",
    )(own, left, right)


def conv_kernel(own, left, right, up, down, kernel, grad, out, pad):
    pad[:MARGIN] = up[...].astype(f32)
    widen(pad.at[MARGIN : MARGIN + TILE_ROWS], slice(0, TILE_ROWS), own, left, right)
    pad[MARGIN + TILE_ROWS :] = down[...].astype(f32)
    total = None
    for col_tap in range(TAPS):
        column = pad[:, TAPS - 1 - col_tap : TAPS - 1 - col_tap + TILE_COLS, :]
        for row_tap in range(TAPS):
            start = TAPS - 1 - row_tap
            n = row_tap * TAPS + col_tap
            term = column[start : start + TILE_ROWS] * kernel[n : n + 1, :][None]
            total = term if total is None else total + term
    out[...] = (grad[...].astype(f32) + total).astype(bf16)


def convolution(own, left, right, up, down, kernel, grad):
    width = 128

    def spec(shape):
        lead = (0,) * (len(shape) - 1)
        return pl.BlockSpec((*shape[:-1], width), lambda i: (*lead, i))

    operands = [own, left, right, up, down, kernel, grad]
    return pl.pallas_call(
        conv_kernel,
        grid=(CHAN // width,),
        out_shape=jax.ShapeDtypeStruct(grad.shape, bf16),
        in_specs=[spec(v.shape) for v in operands],
        out_specs=spec(grad.shape),
        scratch_shapes=[pltpu.VMEM((14, 24, width), f32)],
        compiler_params=pltpu.CompilerParams(vmem_limit_bytes=8 * 2**20),
        name="convolution",
    )(*operands)


def place(where, d, k, r):
    y, c = where[0], where[1]
    row = (k // 4 * 8 + lax.rem(y + r, NY) * 2 + lax.rem(c + d, 2)) * ROWS
    return pl.multiple_of(row, 32), slice(k % 4 * COLS, k % 4 * COLS + COLS)


def own_row(j, c):
    return pl.multiple_of((2 * j + c) * ROWS, 32)


def token_kernel(where, *refs):
    tok, (xs, mine, other, xt) = refs[:NX], refs[NX:]
    c = where[1]
    for i in range(NX):
        rows = slice(i * BLOCK, (i + 1) * BLOCK)
        xs[0, rows, :] = tok[i][:BLOCK]
        xs[1, rows, :] = tok[i][BLOCK:]
    for m in range(2):
        for i in range(CHAN // 256):
            xt[i * 256 : (i + 1) * 256, :] = xs[m, :, i * 256 : (i + 1) * 256].T
        for out, core in ((mine, c), (other, 1 - c)):
            for j in range(PLANES):
                row = own_row(j, core)
                row2 = pl.multiple_of(row + AY, 32)
                out[m, j * AY : (j + 1) * AY, :] = xt[pl.ds(row, AY), :]
                start = PLANES * AY + j * BY
                out[m, start : start + BY, :] = xt[pl.ds(row2, BY), :]


def tokens(where, tok):
    half = jax.ShapeDtypeStruct((2, CHAN // 2, TOKENS), bf16)
    return pl.pallas_call(
        token_kernel,
        out_shape=[jax.ShapeDtypeStruct((2, TOKENS, CHAN), bf16), half, half],
        in_specs=[pl.BlockSpec(memory_space=pltpu.SMEM)] + vmem_specs(NX),
        out_specs=vmem_specs(3),
        scratch_shapes=[pltpu.VMEM((CHAN, TOKENS), bf16)],
        compiler_params=pltpu.CompilerParams(vmem_limit_bytes=20 * 2**20),
        cost_estimate=pl.CostEstimate(flops=0, bytes_accessed=12_000_000, transcendentals=0),
        name="tokens",
    )(where, *tok)


def activation_kernel(where, *refs):
    bias, xs = refs[:2]
    first = refs[2:4]
    second = refs[4 : 4 + NY], refs[4 + NY : 4 + 2 * NY]
    act, pre_grad, w_in, w_out = refs[4 + 2 * NY :]
    for d in range(2):
        for k in range(NZ):
            for r in range(NY):
                row, col = place(where, d, k, r)
                row2 = pl.multiple_of(row + AY, 32)
                for m, w in ((0, w_in), (1, w_out)):
                    w[pl.ds(row, AY), col] = first[d][k, r, m]
                    w[pl.ds(row2, BY), col] = second[d][r][k, m]

    width = 256

    def step(i, _):
        cols = pl.ds(pl.multiple_of(i * width, width), width)
        pre = jnp.dot(xs[0], w_in[:, cols], preferred_element_type=f32) + bias[:, cols]
        back = jnp.dot(xs[1], w_out[:, cols], preferred_element_type=f32)
        cdf = 0.5 * (1.0 + lax.erf(pre * root_half))
        slope = cdf + pre * jnp.exp(-0.5 * pre * pre) * density_norm
        act[:, cols] = (pre * cdf).astype(bf16)
        pre_grad[:, cols] = (back * slope).astype(bf16)
        return 0

    lax.fori_loop(0, HIDDEN // width, step, 0)


def activations(where, bias, xs, first, second):
    operands = [bias, xs, *first, *second[0], *second[1]]
    out = jax.ShapeDtypeStruct((TOKENS, HIDDEN), bf16)
    return pl.pallas_call(
        activation_kernel,
        out_shape=[out, out, jax.ShapeDtypeStruct((CHAN, HIDDEN), bf16)],
        in_specs=[pl.BlockSpec(memory_space=pltpu.SMEM)] + vmem_specs(len(operands)),
        out_specs=vmem_specs(3),
        scratch_shapes=[pltpu.VMEM((CHAN, HIDDEN), bf16)],
        compiler_params=pltpu.CompilerParams(vmem_limit_bytes=40 * 2**20),
        cost_estimate=pl.CostEstimate(
            flops=4 * TOKENS * CHAN * HIDDEN, bytes_accessed=25_000_000, transcendentals=0
        ),
        name="activations",
    )(where, *operands)


def normed_kernel(pre_grad, w_in, *outs):
    width = 256

    def step(i, _):
        cols = pl.ds(pl.multiple_of(i * width, width), width)
        part = lax.dot_general(
            pre_grad[...], w_in[cols, :], (((1,), (1,)), ((), ())), preferred_element_type=f32
        ).astype(bf16)
        for b in range(NX):
            outs[b][:, cols] = part[b * BLOCK : (b + 1) * BLOCK]
        return 0

    lax.fori_loop(0, CHAN // width, step, 0)


def normed_gradient(pre_grad, w_in):
    return pl.pallas_call(
        normed_kernel,
        out_shape=[jax.ShapeDtypeStruct((BLOCK, CHAN), bf16)] * NX,
        in_specs=vmem_specs(2),
        out_specs=vmem_specs(NX),
        compiler_params=pltpu.CompilerParams(vmem_limit_bytes=20 * 2**20),
        cost_estimate=pl.CostEstimate(
            flops=2 * TOKENS * CHAN * HIDDEN, bytes_accessed=20_000_000, transcendentals=0
        ),
        name="normed_gradient",
    )(pre_grad, w_in)


def weight_kernel(y_first, where, mine, got, *refs):
    sides, outs, g = (refs[0:2], refs[2:4]), refs[4:-1], refs[-1]
    rows = slice(PLANES * AY, CHAN // 2) if y_first else slice(0, PLANES * AY)
    height = BY if y_first else AY
    width = 256
    for m in range(2):
        own, other = sides[m]

        def step(i, _, m=m, own=own, other=other):
            cols = pl.ds(pl.multiple_of(i * width, width), width)
            value = jnp.dot(mine[m, rows], own[:, cols], preferred_element_type=f32)
            value = value + jnp.dot(got[m, rows], other[:, cols], preferred_element_type=f32)
            g[:, cols] = value.astype(bf16)
            return 0

        lax.fori_loop(0, HIDDEN // width, step, 0)
        for k in range(NZ):
            col = slice(k % 4 * COLS, k % 4 * COLS + COLS)
            for r in range(NY):
                j = k // 4 * NY + lax.rem(where[0] + r, NY)
                piece = g[pl.ds(pl.multiple_of(j * height, 32), height), col]
                if y_first:
                    outs[r][k, m] = piece
                else:
                    outs[0][k, r, m] = piece


def weight_gradients(y_first, where, *operands):
    if y_first:
        outs = [jax.ShapeDtypeStruct((NZ, 2, BY, COLS), bf16)] * NY
    else:
        outs = [jax.ShapeDtypeStruct((NZ, NY, 2, AY, COLS), bf16)]
    height = PLANES * (BY if y_first else AY)
    return pl.pallas_call(
        functools.partial(weight_kernel, y_first),
        out_shape=outs,
        in_specs=[pl.BlockSpec(memory_space=pltpu.SMEM)] + vmem_specs(len(operands)),
        out_specs=vmem_specs(len(outs)),
        scratch_shapes=[pltpu.VMEM((height, HIDDEN), bf16)],
        compiler_params=pltpu.CompilerParams(vmem_limit_bytes=28 * 2**20),
        cost_estimate=pl.CostEstimate(
            flops=8 * TOKENS * height * HIDDEN, bytes_accessed=20_000_000, transcendentals=0
        ),
        name="weight_gradients",
    )(where, *operands)


def sum_y_kernel(*refs):
    for k in range(NZ):
        total = refs[0][k].astype(f32)
        for ref in refs[1:NY]:
            total = total + ref[k].astype(f32)
        refs[NY][k] = total.astype(bf16)


def sum_y(parts):
    vmem = pl.BlockSpec(memory_space=pltpu.VMEM)
    return pl.pallas_call(
        sum_y_kernel,
        out_shape=jax.ShapeDtypeStruct(parts[0].shape, bf16),
        in_specs=[vmem] * NY,
        out_specs=vmem,
        compiler_params=pltpu.CompilerParams(vmem_limit_bytes=24 * 2**20),
        name="sum_y",
    )(*parts)


def sum_z_kernel(parts, *outs):
    for r in range(NY):
        total = parts[0, r].astype(f32)
        for k in range(1, NZ):
            total = total + parts[k, r].astype(f32)
        outs[r][...] = total.astype(bf16)


def sum_z(parts):
    vmem = pl.BlockSpec(memory_space=pltpu.VMEM)
    return pl.pallas_call(
        sum_z_kernel,
        out_shape=[jax.ShapeDtypeStruct(parts.shape[2:], bf16)] * NY,
        in_specs=[vmem],
        out_specs=[vmem] * NY,
        compiler_params=pltpu.CompilerParams(vmem_limit_bytes=24 * 2**20),
        name="sum_z",
    )(parts)


def finish_kernel(*refs):
    zs, (ys, grad_in, grad_out) = refs[:NY], refs[NY:]
    factor = 1.0 / math.sqrt(BLOCK * 256)
    for m in range(2):
        lead = zs[0][m].astype(f32)
        for part in zs[1:]:
            lead = lead + part[m].astype(f32)
        rest = ys[0, m].astype(f32)
        for k in range(1, NZ):
            rest = rest + ys[k, m].astype(f32)
        value = jnp.concatenate([lead, rest]) * factor
        if m == 0:
            grad_in[...] = value
        else:
            grad_out[...] = value.T


def finish(zs, ys):
    return pl.pallas_call(
        finish_kernel,
        out_shape=[
            jax.ShapeDtypeStruct((ROWS, COLS), f32),
            jax.ShapeDtypeStruct((COLS, ROWS), f32),
        ],
        in_specs=vmem_specs(NY + 1),
        out_specs=vmem_specs(2),
        compiler_params=pltpu.CompilerParams(vmem_limit_bytes=8 * 2**20),
        name="finish",
    )(*zs, ys)


def body(
    conv_out, out_grad, layer_norm_gain, layer_norm_bias, w_in, b_in, w_out, layer_scale, dw_kernel
):
    gain, shift_row, scale = (
        v.reshape(1, CHAN) for v in (layer_norm_gain, layer_norm_bias, layer_scale)
    )
    token, xhat, inverse = layer_norm(
        conv_out.reshape(BLOCK, CHAN), out_grad.reshape(BLOCK, CHAN), gain, shift_row, scale
    )

    shards = jnp.stack([w_in, w_out.T])
    lead, rest = shards[:, :AY], shards[:, AY:]
    load = jnp.concatenate([rest.reshape(2 * BY, COLS), bias_rows(b_in)])
    load, token = lax.optimization_barrier((load, token))
    tok = [to_x(token, -r) for r in range(NX)]
    got = gather_z(load)
    lead_y = jnp.stack([to_y(lead, -r) for r in range(NY)])
    got, lead_y, tok[1], tok[3] = lax.optimization_barrier((got, lead_y, tok[1], tok[3]))
    rest_z = got[:, : 2 * BY].reshape(NZ, 2, BY, COLS)
    bias = jnp.sum(got[:4, 2 * BY : 2 * BY + 3].astype(f32), axis=1).reshape(1, HIDDEN)
    second = [to_y(rest_z, -r) for r in range(NY)]
    first = gather_z(lead_y)
    swapped = [swap(v) for v in second[:2]] + [None, swap(second[3])]
    where = jnp.stack([lax.axis_index("y"), lax.axis_index("c")]).astype(jnp.int32)
    first, swapped[1], swapped[3], second[2], tok[2] = lax.optimization_barrier(
        (first, swapped[1], swapped[3], second[2], tok[2])
    )
    xs, mine, other = tokens(where, tok)
    other = swap(other)
    swapped[2] = swap(second[2])
    second = [second, swapped]
    first = [first, swap(first)]

    act, pre_grad, w_all = activations(where, bias, xs, first, second)
    other_act, other_pre_grad = swap(act), swap(pre_grad)
    part = normed_gradient(pre_grad, w_all)
    other_act, other_pre_grad, *part = lax.optimization_barrier(
        (other_act, other_pre_grad, *part)
    )
    part = [to_x(v, r) for r, v in enumerate(part)]
    operands = [mine, other, pre_grad, other_pre_grad, act, other_act]
    zs = weight_gradients(False, where, *operands)[0]
    *operands, zs = lax.optimization_barrier((*operands, zs))
    ys = weight_gradients(True, where, *operands)
    ys = [to_y(v, r) for r, v in enumerate(ys)]
    own, first_cols, last_cols = layer_norm_backward(part, xhat, inverse, gain)
    left, right = to_tile(last_cols, 0, 1), to_tile(first_cols, 0, -1)
    ys = sum_y(ys)
    ys, own, left, right = lax.optimization_barrier((ys, own, left, right))
    zs = sum_z(exchange_z(zs))
    left, right, *zs = lax.optimization_barrier((left, right, *zs))
    first_rows, last_rows = edges(own, left, right)
    up, down = to_tile(last_rows, 1, 0), to_tile(first_rows, -1, 0)
    zs = [to_y(v, r) for r, v in enumerate(zs)]
    ys = exchange_z(ys)
    kernel = dw_kernel.reshape(TAPS * TAPS, CHAN)
    grad_input = convolution(own, left, right, up, down, kernel, out_grad)
    grad_input, ys = lax.optimization_barrier((grad_input, ys))
    grad_in, grad_out = finish(zs, ys)
    return (grad_input, grad_in, grad_out)


def solution(mesh):
    fine = Mesh(mesh.devices.reshape(SIZES), FINE)
    token = P(STRIP, TENSOR, None)
    return jax.shard_map(
        body,
        mesh=fine,
        in_specs=(
            token,
            token,
            P(),
            P(),
            P(STRIP, TENSOR),
            P(TENSOR),
            P(TENSOR, STRIP),
            P(),
            P(),
        ),
        out_specs=(token, P(STRIP, TENSOR), P(TENSOR, STRIP)),
        check_vma=False,
    )
```

```python
import math

import jax
import jax.numpy as jnp
from jax import lax
from jax.experimental import pallas as pl
from jax.experimental.pallas import tpu as pltpu
from jax.sharding import Mesh
from jax.sharding import PartitionSpec as P

ln_eps = 1e-06
root_half = 0.7071067811865476
density_norm = 0.3989422804014327

FINE = ("zl", "y", "c", "x", "zh")
SIZES = (2, 4, 2, 4, 4)
STRIP = ("zl", "y", "c")
TENSOR = ("x", "zh")
Z = ("zl", "zh")
NX, NY, NZ = 4, 4, 8
CHAN, HIDDEN = 1536, 1536
ROWS, COLS = 96, 384
PLANES = 8
AY, BY = 32, 64
BLOCK = 128
TOKENS = BLOCK * NX

bf16, f32 = jnp.bfloat16, jnp.float32


def shift(n, k):
    return [(i, (i + k) % n) for i in range(n)]


def to_x(value, k):
    return lax.ppermute(value, "x", shift(NX, k)) if k else value


def to_y(value, k):
    return lax.ppermute(value, "y", shift(NY, k)) if k else value


def exchange_z(value):
    return lax.all_to_all(value, Z, 0, 0, tiled=True)


def bias_rows(bias):
    rows = []
    for _ in range(3):
        term = lax.reduce_precision(bias, 8, 7)
        rows.append(term.astype(bf16))
        bias = bias - term
    return jnp.concatenate([jnp.stack(rows), jnp.zeros((13, COLS), bf16)])


def gather_z(value):
    return exchange_z(jnp.broadcast_to(value, (NZ, *value.shape)))


def swap(value):
    return lax.ppermute(value, "c", shift(2, 1))


TILE_ROWS, TILE_COLS, TAPS, MARGIN = 8, 16, 7, 3


def to_tile(value, down, right):
    pairs = [
        (s * 16 + t, (s + down) * 16 + t + right)
        for s in range(16)
        for t in range(16)
        if 0 <= s + down < 16 and 0 <= t + right < 16
    ]
    return lax.ppermute(value, FINE, pairs)


def vmem_specs(count):
    return [pl.BlockSpec(memory_space=pltpu.VMEM)] * count


def norm_kernel(x, grad, gain, bias, scale, token, xhat, inverse):
    for i in range(0, BLOCK, 16):
        rows = slice(i, i + 16)
        value = x[rows].astype(f32)
        value = value - jnp.mean(value, axis=-1, keepdims=True)
        inv = lax.rsqrt(jnp.mean(value * value, axis=-1, keepdims=True) + ln_eps)
        value = value * inv
        xhat[rows] = value
        inverse[rows] = inv
        token[rows] = (value * gain[...] + bias[...]).astype(bf16)
        token[i + BLOCK : i + BLOCK + 16] = (grad[rows].astype(f32) * scale[...]).astype(bf16)


def layer_norm(x, grad, gain, bias, scale):
    return pl.pallas_call(
        norm_kernel,
        out_shape=[
            jax.ShapeDtypeStruct((2 * BLOCK, CHAN), bf16),
            jax.ShapeDtypeStruct((BLOCK, CHAN), f32),
            jax.ShapeDtypeStruct((BLOCK, 1), f32),
        ],
        in_specs=vmem_specs(5),
        out_specs=vmem_specs(3),
        compiler_params=pltpu.CompilerParams(vmem_limit_bytes=16 * 2**20),
        name="layer_norm",
    )(x, grad, gain, bias, scale)


def norm_backward_kernel(*refs):
    parts, (xhat, inverse, gain, out, first_cols, last_cols) = refs[:NX], refs[NX:]
    for i in range(TILE_ROWS):
        rows = slice(i * TILE_COLS, (i + 1) * TILE_COLS)
        value = parts[0][rows].astype(f32)
        for part in parts[1:]:
            value = value + part[rows].astype(f32)
        value = value * gain[...]
        hat = xhat[rows]
        first = jnp.mean(value, axis=-1, keepdims=True)
        second = jnp.mean(value * hat, axis=-1, keepdims=True)
        value = inverse[rows] * (value - first - hat * second)
        out[i] = value.astype(bf16)
        first_cols[i] = value[:MARGIN].astype(bf16)
        last_cols[i] = value[TILE_COLS - MARGIN :].astype(bf16)


def layer_norm_backward(parts, xhat, inverse, gain):
    return pl.pallas_call(
        norm_backward_kernel,
        out_shape=[jax.ShapeDtypeStruct((TILE_ROWS, TILE_COLS, CHAN), bf16)]
        + [jax.ShapeDtypeStruct((TILE_ROWS, MARGIN, CHAN), bf16)] * 2,
        in_specs=vmem_specs(NX + 3),
        out_specs=vmem_specs(3),
        compiler_params=pltpu.CompilerParams(vmem_limit_bytes=16 * 2**20),
        name="layer_norm_backward",
    )(*parts, xhat, inverse, gain)


def widen(out, rows, own, left, right):
    out[:, :MARGIN] = left[rows].astype(out.dtype)
    out[:, MARGIN : MARGIN + TILE_COLS] = own[rows].astype(out.dtype)
    out[:, MARGIN + TILE_COLS : TILE_COLS + 2 * MARGIN] = right[rows].astype(out.dtype)


def edge_kernel(own, left, right, first_rows, last_rows, scratch):
    for out, rows in ((first_rows, slice(0, 3)), (last_rows, slice(5, 8))):
        scratch[:, 16:, :] = jnp.zeros((MARGIN, 8, CHAN), f32)
        widen(scratch, rows, own, left, right)
        out[...] = scratch[...].astype(bf16)


def edges(own, left, right):
    return pl.pallas_call(
        edge_kernel,
        out_shape=[jax.ShapeDtypeStruct((MARGIN, 24, CHAN), bf16)] * 2,
        in_specs=vmem_specs(3),
        out_specs=vmem_specs(2),
        scratch_shapes=[pltpu.VMEM((MARGIN, 24, CHAN), f32)],
        compiler_params=pltpu.CompilerParams(vmem_limit_bytes=8 * 2**20),
        name="edges",
    )(own, left, right)


def conv_kernel(own, left, right, up, down, kernel, grad, out, pad):
    pad[:MARGIN] = up[...].astype(f32)
    widen(pad.at[MARGIN : MARGIN + TILE_ROWS], slice(0, TILE_ROWS), own, left, right)
    pad[MARGIN + TILE_ROWS :] = down[...].astype(f32)
    total = None
    for col_tap in range(TAPS):
        column = pad[:, TAPS - 1 - col_tap : TAPS - 1 - col_tap + TILE_COLS, :]
        for row_tap in range(TAPS):
            start = TAPS - 1 - row_tap
            term = column[start : start + TILE_ROWS] * kernel[row_tap, col_tap : col_tap + 1, :][None]
            total = term if total is None else total + term
    out[...] = (grad[...].astype(f32) + total).astype(bf16)


def convolution(own, left, right, up, down, kernel, grad):
    width = 128

    def spec(shape):
        lead = (0,) * (len(shape) - 1)
        return pl.BlockSpec((*shape[:-1], width), lambda i: (*lead, i))

    operands = [own, left, right, up, down, kernel, grad]
    return pl.pallas_call(
        conv_kernel,
        grid=(CHAN // width,),
        out_shape=jax.ShapeDtypeStruct(grad.shape, bf16),
        in_specs=[spec(v.shape) for v in operands],
        out_specs=spec(grad.shape),
        scratch_shapes=[pltpu.VMEM((14, 24, width), f32)],
        compiler_params=pltpu.CompilerParams(vmem_limit_bytes=8 * 2**20),
        name="convolution",
    )(*operands)


def place(where, d, k, r):
    y, c = where[0], where[1]
    row = (k // 4 * 8 + lax.rem(y + r, NY) * 2 + lax.rem(c + d, 2)) * ROWS
    return pl.multiple_of(row, 32), slice(k % 4 * COLS, k % 4 * COLS + COLS)


def own_row(j, c):
    return pl.multiple_of((2 * j + c) * ROWS, 32)


def token_kernel(where, *refs):
    tok, (xs, mine, other, xt, sems) = refs[:NX], refs[NX:]
    c = where[1]
    copies = [
        [
            pltpu.make_async_copy(
                tok[i].at[pl.ds(m * BLOCK, BLOCK)],
                xs.at[m, pl.ds(i * BLOCK, BLOCK)],
                sems.at[m, i],
            )
            for i in range(NX)
        ]
        for m in range(2)
    ]
    for m in range(2):
        for i in range(NX):
            copies[m][i].start()
    for m in range(2):
        for i in range(NX):
            copies[m][i].wait()
        for i in range(CHAN // 256):
            xt[i * 256 : (i + 1) * 256, :] = xs[m, :, i * 256 : (i + 1) * 256].T
        for out, core in ((mine, c), (other, 1 - c)):
            for j in range(PLANES):
                row = own_row(j, core)
                row2 = pl.multiple_of(row + AY, 32)
                out[m, j * AY : (j + 1) * AY, :] = xt[pl.ds(row, AY), :]
                start = PLANES * AY + j * BY
                out[m, start : start + BY, :] = xt[pl.ds(row2, BY), :]


def tokens(where, tok):
    half = jax.ShapeDtypeStruct((2, CHAN // 2, TOKENS), bf16)
    return pl.pallas_call(
        token_kernel,
        out_shape=[jax.ShapeDtypeStruct((2, TOKENS, CHAN), bf16), half, half],
        in_specs=[pl.BlockSpec(memory_space=pltpu.SMEM)]
        + [pl.BlockSpec(memory_space=pl.ANY)] * NX,
        out_specs=vmem_specs(3),
        scratch_shapes=[pltpu.VMEM((CHAN, TOKENS), bf16), pltpu.SemaphoreType.DMA((2, NX))],
        compiler_params=pltpu.CompilerParams(vmem_limit_bytes=20 * 2**20),
        cost_estimate=pl.CostEstimate(flops=0, bytes_accessed=12_000_000, transcendentals=0),
        name="tokens",
    )(where, *tok)


def activation_kernel(where, *refs):
    bias, xs = refs[:2]
    first = refs[2:4]
    second = refs[4 : 4 + NY], refs[4 + NY : 4 + 2 * NY]
    act, pre_grad, w_in, w_out = refs[4 + 2 * NY :]
    for d in range(2):
        for k in range(NZ):
            for r in range(NY):
                row, col = place(where, d, k, r)
                row2 = pl.multiple_of(row + AY, 32)
                for m, w in ((0, w_in), (1, w_out)):
                    w[pl.ds(row, AY), col] = first[d][k, r, m]
                    w[pl.ds(row2, BY), col] = second[d][r][k, m]

    width = 256

    def products(i):
        cols = slice(i * width, (i + 1) * width)
        pre = jnp.dot(xs[0], w_in[:, cols], preferred_element_type=f32) + bias[:, cols]
        return pre, jnp.dot(xs[1], w_out[:, cols], preferred_element_type=f32)

    count = HIDDEN // width
    pre, back = products(0)
    for i in range(count):
        following = products(i + 1) if i + 1 < count else None
        cols = slice(i * width, (i + 1) * width)
        cdf = 0.5 * (1.0 + lax.erf(pre * root_half))
        slope = cdf + pre * jnp.exp(-0.5 * pre * pre) * density_norm
        act[:, cols] = (pre * cdf).astype(bf16)
        pre_grad[:, cols] = (back * slope).astype(bf16)
        if following is not None:
            pre, back = following


def activations(where, bias, xs, first, second):
    operands = [bias, xs, *first, *second[0], *second[1]]
    out = jax.ShapeDtypeStruct((TOKENS, HIDDEN), bf16)
    return pl.pallas_call(
        activation_kernel,
        out_shape=[out, out, jax.ShapeDtypeStruct((CHAN, HIDDEN), bf16)],
        in_specs=[pl.BlockSpec(memory_space=pltpu.SMEM)] + vmem_specs(len(operands)),
        out_specs=vmem_specs(3),
        scratch_shapes=[pltpu.VMEM((CHAN, HIDDEN), bf16)],
        compiler_params=pltpu.CompilerParams(vmem_limit_bytes=40 * 2**20),
        cost_estimate=pl.CostEstimate(
            flops=4 * TOKENS * CHAN * HIDDEN, bytes_accessed=25_000_000, transcendentals=0
        ),
        name="activations",
    )(where, *operands)


def normed_kernel(pre_grad, w_in, *outs):
    part = lax.dot_general(
        pre_grad[...], w_in[...], (((1,), (1,)), ((), ())), preferred_element_type=f32
    ).astype(bf16)
    for b in range(NX):
        outs[b][...] = part[b * BLOCK : (b + 1) * BLOCK]


def normed_gradient(pre_grad, w_in):
    width = 256
    return pl.pallas_call(
        normed_kernel,
        grid=(CHAN // width,),
        out_shape=[jax.ShapeDtypeStruct((BLOCK, CHAN), bf16)] * NX,
        in_specs=[
            pl.BlockSpec((TOKENS, HIDDEN), lambda i: (0, 0)),
            pl.BlockSpec((width, HIDDEN), lambda i: (i, 0)),
        ],
        out_specs=[pl.BlockSpec((BLOCK, width), lambda i: (0, i))] * NX,
        compiler_params=pltpu.CompilerParams(vmem_limit_bytes=20 * 2**20),
        cost_estimate=pl.CostEstimate(
            flops=2 * TOKENS * CHAN * HIDDEN, bytes_accessed=20_000_000, transcendentals=0
        ),
        name="normed_gradient",
    )(pre_grad, w_in)


def weight_kernel(where, mine, got, *refs):
    sides, (ys, out_z, g) = (refs[0:2], refs[2:4]), (refs[4 : 4 + NY], *refs[4 + NY :])
    width = 256
    for m in range(2):
        own, other = sides[m]

        def step(i, _, m=m, own=own, other=other):
            cols = pl.ds(pl.multiple_of(i * width, width), width)
            value = jnp.dot(mine[m], own[:, cols], preferred_element_type=f32)
            value = value + jnp.dot(got[m], other[:, cols], preferred_element_type=f32)
            g[:, cols] = value.astype(bf16)
            return 0

        lax.fori_loop(0, HIDDEN // width, step, 0)
        for k in range(NZ):
            col = slice(k % 4 * COLS, k % 4 * COLS + COLS)
            for r in range(NY):
                j = k // 4 * NY + lax.rem(where[0] + r, NY)
                row = pl.multiple_of(j * AY, 32)
                row2 = pl.multiple_of(PLANES * AY + j * BY, 32)
                out_z[k, r, m] = g[pl.ds(row, AY), col]
                ys[r][k, m] = g[pl.ds(row2, BY), col]


def weight_gradients(where, mine, got, pre_grad, other_pre_grad, act, other_act):
    operands = [mine, got, pre_grad, other_pre_grad, act, other_act]
    out = pl.pallas_call(
        weight_kernel,
        out_shape=[jax.ShapeDtypeStruct((NZ, 2, BY, COLS), bf16)] * NY
        + [jax.ShapeDtypeStruct((NZ, NY, 2, AY, COLS), bf16)],
        in_specs=[pl.BlockSpec(memory_space=pltpu.SMEM)] + vmem_specs(len(operands)),
        out_specs=vmem_specs(NY + 1),
        scratch_shapes=[pltpu.VMEM((CHAN // 2, HIDDEN), bf16)],
        compiler_params=pltpu.CompilerParams(vmem_limit_bytes=32 * 2**20),
        cost_estimate=pl.CostEstimate(
            flops=4 * TOKENS * CHAN * HIDDEN, bytes_accessed=30_000_000, transcendentals=0
        ),
        name="weight_gradients",
    )(where, *operands)
    return out[:NY], out[NY]


def sum_y_kernel(*refs):
    for k in range(NZ):
        total = refs[0][k].astype(f32)
        for ref in refs[1:NY]:
            total = total + ref[k].astype(f32)
        refs[NY][k] = total.astype(bf16)


def sum_y(parts):
    vmem = pl.BlockSpec(memory_space=pltpu.VMEM)
    return pl.pallas_call(
        sum_y_kernel,
        out_shape=jax.ShapeDtypeStruct(parts[0].shape, bf16),
        in_specs=[vmem] * NY,
        out_specs=vmem,
        compiler_params=pltpu.CompilerParams(vmem_limit_bytes=24 * 2**20),
        name="sum_y",
    )(*parts)


def sum_z_kernel(parts, *outs):
    for r in range(NY):
        total = parts[0, r].astype(f32)
        for k in range(1, NZ):
            total = total + parts[k, r].astype(f32)
        outs[r][...] = total.astype(bf16)


def sum_z(parts):
    vmem = pl.BlockSpec(memory_space=pltpu.VMEM)
    return pl.pallas_call(
        sum_z_kernel,
        out_shape=[jax.ShapeDtypeStruct(parts.shape[2:], bf16)] * NY,
        in_specs=[vmem],
        out_specs=[vmem] * NY,
        compiler_params=pltpu.CompilerParams(vmem_limit_bytes=24 * 2**20),
        name="sum_z",
    )(parts)


def finish_kernel(*refs):
    zs, (ys, grad_in, grad_out) = refs[:NY], refs[NY:]
    factor = 1.0 / math.sqrt(BLOCK * 256)
    for m in range(2):
        lead = zs[0][m].astype(f32)
        for part in zs[1:]:
            lead = lead + part[m].astype(f32)
        rest = ys[0, m].astype(f32)
        for k in range(1, NZ):
            rest = rest + ys[k, m].astype(f32)
        value = jnp.concatenate([lead, rest]) * factor
        if m == 0:
            grad_in[...] = value
        else:
            grad_out[...] = value.T


def finish(zs, ys):
    return pl.pallas_call(
        finish_kernel,
        out_shape=[
            jax.ShapeDtypeStruct((ROWS, COLS), f32),
            jax.ShapeDtypeStruct((COLS, ROWS), f32),
        ],
        in_specs=vmem_specs(NY + 1),
        out_specs=vmem_specs(2),
        compiler_params=pltpu.CompilerParams(vmem_limit_bytes=8 * 2**20),
        name="finish",
    )(*zs, ys)


def body(
    conv_out, out_grad, layer_norm_gain, layer_norm_bias, w_in, b_in, w_out, layer_scale, dw_kernel
):
    gain, shift_row, scale = (
        v.reshape(1, CHAN) for v in (layer_norm_gain, layer_norm_bias, layer_scale)
    )
    token, xhat, inverse = layer_norm(
        conv_out.reshape(BLOCK, CHAN), out_grad.reshape(BLOCK, CHAN), gain, shift_row, scale
    )
    tok = [to_x(token, -r) for r in range(NX)]

    shards = jnp.stack([w_in, w_out.T])
    lead, rest = shards[:, :AY], shards[:, AY:]
    got = gather_z(jnp.concatenate([rest.reshape(2 * BY, COLS), bias_rows(b_in)]))
    lead_y = jnp.stack([to_y(lead, -r) for r in range(NY)])
    got, lead_y, tok[1], tok[3] = lax.optimization_barrier((got, lead_y, tok[1], tok[3]))
    rest_z = got[:, : 2 * BY].reshape(NZ, 2, BY, COLS)
    bias = jnp.sum(got[:4, 2 * BY : 2 * BY + 3].astype(f32), axis=1).reshape(1, HIDDEN)
    second = [to_y(rest_z, -r) for r in range(NY)]
    first = gather_z(lead_y)
    swapped = [swap(v) for v in second[:2]] + [None, swap(second[3])]
    where = jnp.stack([lax.axis_index("y"), lax.axis_index("c")]).astype(jnp.int32)
    first, swapped[1], swapped[3], second[2], tok[2] = lax.optimization_barrier(
        (first, swapped[1], swapped[3], second[2], tok[2])
    )
    xs, mine, other = tokens(where, tok)
    other = swap(other)
    swapped[2] = swap(second[2])
    second = [second, swapped]
    first = [first, swap(first)]

    act, pre_grad, w_all = activations(where, bias, xs, first, second)
    other_act, other_pre_grad = swap(act), swap(pre_grad)
    part = normed_gradient(pre_grad, w_all)
    other_act, other_pre_grad, *part = lax.optimization_barrier(
        (other_act, other_pre_grad, *part)
    )
    part = [to_x(v, r) for r, v in enumerate(part)]
    ys, zs = weight_gradients(where, mine, other, pre_grad, other_pre_grad, act, other_act)
    ys = [to_y(v, r) for r, v in enumerate(ys)]
    own, first_cols, last_cols = layer_norm_backward(part, xhat, inverse, gain)
    left, right = to_tile(last_cols, 0, 1), to_tile(first_cols, 0, -1)
    ys = sum_y(ys)
    ys, own, left, right = lax.optimization_barrier((ys, own, left, right))
    zs = sum_z(exchange_z(zs))
    left, right, *zs = lax.optimization_barrier((left, right, *zs))
    first_rows, last_rows = edges(own, left, right)
    up, down = to_tile(last_rows, 1, 0), to_tile(first_rows, -1, 0)
    zs = [to_y(v, r) for r, v in enumerate(zs)]
    ys = exchange_z(ys)
    grad_input = convolution(own, left, right, up, down, dw_kernel, out_grad)
    grad_input, ys = lax.optimization_barrier((grad_input, ys))
    grad_in, grad_out = finish(zs, ys)
    return (grad_input, grad_in, grad_out)


def solution(mesh):
    fine = Mesh(mesh.devices.reshape(SIZES), FINE)
    token = P(STRIP, TENSOR, None)
    return jax.shard_map(
        body,
        mesh=fine,
        in_specs=(
            token,
            token,
            P(),
            P(),
            P(STRIP, TENSOR),
            P(TENSOR),
            P(TENSOR, STRIP),
            P(),
            P(),
        ),
        out_specs=(token, P(STRIP, TENSOR), P(TENSOR, STRIP)),
        check_vma=False,
    )
```

```python
import math

import jax
import jax.numpy as jnp
from jax import lax
from jax.experimental import pallas as pl
from jax.experimental.pallas import tpu as pltpu
from jax.sharding import Mesh
from jax.sharding import PartitionSpec as P

ln_eps = 1e-06
root_half = 0.7071067811865476
density_norm = 0.3989422804014327

FINE = ("zl", "y", "c", "x", "zh")
SIZES = (2, 4, 2, 4, 4)
STRIP = ("zl", "y", "c")
TENSOR = ("x", "zh")
Z = ("zl", "zh")
NX, NY, NZ = 4, 4, 8
CHAN, HIDDEN = 1536, 1536
ROWS, COLS = 96, 384
PLANES = 8
AY, BY = 32, 64
BLOCK = 128
TOKENS = BLOCK * NX

bf16, f32 = jnp.bfloat16, jnp.float32


def shift(n, k):
    return [(i, (i + k) % n) for i in range(n)]


def to_x(value, k):
    return lax.ppermute(value, "x", shift(NX, k)) if k else value


def to_y(value, k):
    return lax.ppermute(value, "y", shift(NY, k)) if k else value


def exchange_z(value):
    return lax.all_to_all(value, Z, 0, 0, tiled=True)


def bias_rows(bias):
    rows = []
    for _ in range(3):
        term = lax.reduce_precision(bias, 8, 7)
        rows.append(term.astype(bf16))
        bias = bias - term
    return jnp.concatenate([jnp.stack(rows), jnp.zeros((13, COLS), bf16)])


def gather_z(value):
    return exchange_z(jnp.broadcast_to(value, (NZ, *value.shape)))


def swap(value):
    return lax.ppermute(value, "c", shift(2, 1))


TILE_ROWS, TILE_COLS, TAPS, MARGIN = 8, 16, 7, 3


def to_tile(value, down, right):
    pairs = [
        (s * 16 + t, (s + down) * 16 + t + right)
        for s in range(16)
        for t in range(16)
        if 0 <= s + down < 16 and 0 <= t + right < 16
    ]
    return lax.ppermute(value, FINE, pairs)


def vmem_specs(count):
    return [pl.BlockSpec(memory_space=pltpu.VMEM)] * count


def norm_kernel(x, grad, gain, bias, scale, token, xhat, inverse):
    for i in range(0, BLOCK, 16):
        rows = slice(i, i + 16)
        value = x[rows].astype(f32)
        value = value - jnp.mean(value, axis=-1, keepdims=True)
        inv = lax.rsqrt(jnp.mean(value * value, axis=-1, keepdims=True) + ln_eps)
        value = value * inv
        xhat[rows] = value
        inverse[rows] = inv
        token[rows] = (value * gain[...] + bias[...]).astype(bf16)
        token[i + BLOCK : i + BLOCK + 16] = (grad[rows].astype(f32) * scale[...]).astype(bf16)


def layer_norm(x, grad, gain, bias, scale):
    return pl.pallas_call(
        norm_kernel,
        out_shape=[
            jax.ShapeDtypeStruct((2 * BLOCK, CHAN), bf16),
            jax.ShapeDtypeStruct((BLOCK, CHAN), f32),
            jax.ShapeDtypeStruct((BLOCK, 1), f32),
        ],
        in_specs=vmem_specs(5),
        out_specs=vmem_specs(3),
        compiler_params=pltpu.CompilerParams(vmem_limit_bytes=16 * 2**20),
        name="layer_norm",
    )(x, grad, gain, bias, scale)


def norm_backward_kernel(*refs):
    parts, (xhat, inverse, gain, out, first_cols, last_cols) = refs[:NX], refs[NX:]
    for i in range(TILE_ROWS):
        rows = slice(i * TILE_COLS, (i + 1) * TILE_COLS)
        value = parts[0][rows].astype(f32)
        for part in parts[1:]:
            value = value + part[rows].astype(f32)
        value = value * gain[...]
        hat = xhat[rows]
        first = jnp.mean(value, axis=-1, keepdims=True)
        second = jnp.mean(value * hat, axis=-1, keepdims=True)
        value = inverse[rows] * (value - first - hat * second)
        out[i] = value.astype(bf16)
        first_cols[i] = value[:MARGIN].astype(bf16)
        last_cols[i] = value[TILE_COLS - MARGIN :].astype(bf16)


def layer_norm_backward(parts, xhat, inverse, gain):
    return pl.pallas_call(
        norm_backward_kernel,
        out_shape=[jax.ShapeDtypeStruct((TILE_ROWS, TILE_COLS, CHAN), bf16)]
        + [jax.ShapeDtypeStruct((TILE_ROWS, MARGIN, CHAN), bf16)] * 2,
        in_specs=vmem_specs(NX + 3),
        out_specs=vmem_specs(3),
        compiler_params=pltpu.CompilerParams(vmem_limit_bytes=16 * 2**20),
        name="layer_norm_backward",
    )(*parts, xhat, inverse, gain)


def widen(out, rows, own, left, right):
    out[:, :MARGIN] = left[rows].astype(out.dtype)
    out[:, MARGIN : MARGIN + TILE_COLS] = own[rows].astype(out.dtype)
    out[:, MARGIN + TILE_COLS : TILE_COLS + 2 * MARGIN] = right[rows].astype(out.dtype)


def edge_kernel(own, left, right, first_rows, last_rows, scratch):
    for out, rows in ((first_rows, slice(0, 3)), (last_rows, slice(5, 8))):
        scratch[:, 16:, :] = jnp.zeros((MARGIN, 8, CHAN), f32)
        widen(scratch, rows, own, left, right)
        out[...] = scratch[...].astype(bf16)


def edges(own, left, right):
    return pl.pallas_call(
        edge_kernel,
        out_shape=[jax.ShapeDtypeStruct((MARGIN, 24, CHAN), bf16)] * 2,
        in_specs=vmem_specs(3),
        out_specs=vmem_specs(2),
        scratch_shapes=[pltpu.VMEM((MARGIN, 24, CHAN), f32)],
        compiler_params=pltpu.CompilerParams(vmem_limit_bytes=8 * 2**20),
        name="edges",
    )(own, left, right)


def conv_kernel(own, left, right, up, down, kernel, grad, out, pad):
    pad[:MARGIN] = up[...].astype(f32)
    widen(pad.at[MARGIN : MARGIN + TILE_ROWS], slice(0, TILE_ROWS), own, left, right)
    pad[MARGIN + TILE_ROWS :] = down[...].astype(f32)
    total = None
    for col_tap in range(TAPS):
        column = pad[:, TAPS - 1 - col_tap : TAPS - 1 - col_tap + TILE_COLS, :]
        for row_tap in range(TAPS):
            start = TAPS - 1 - row_tap
            term = column[start : start + TILE_ROWS] * kernel[row_tap, col_tap : col_tap + 1, :][None]
            total = term if total is None else total + term
    out[...] = (grad[...].astype(f32) + total).astype(bf16)


def convolution(own, left, right, up, down, kernel, grad):
    width = 128

    def spec(shape):
        lead = (0,) * (len(shape) - 1)
        return pl.BlockSpec((*shape[:-1], width), lambda i: (*lead, i))

    operands = [own, left, right, up, down, kernel, grad]
    return pl.pallas_call(
        conv_kernel,
        grid=(CHAN // width,),
        out_shape=jax.ShapeDtypeStruct(grad.shape, bf16),
        in_specs=[spec(v.shape) for v in operands],
        out_specs=spec(grad.shape),
        scratch_shapes=[pltpu.VMEM((14, 24, width), f32)],
        compiler_params=pltpu.CompilerParams(vmem_limit_bytes=8 * 2**20),
        name="convolution",
    )(*operands)


def place(where, d, k, r):
    y, c = where[0], where[1]
    row = (k // 4 * 8 + lax.rem(y + r, NY) * 2 + lax.rem(c + d, 2)) * ROWS
    return pl.multiple_of(row, 32), slice(k % 4 * COLS, k % 4 * COLS + COLS)


def own_row(j, c):
    return pl.multiple_of((2 * j + c) * ROWS, 32)


def token_kernel(where, *refs):
    tok, (xs, mine, other, xt, sems) = refs[:NX], refs[NX:]
    c = where[1]
    copies = [
        [
            pltpu.make_async_copy(
                tok[i].at[pl.ds(m * BLOCK, BLOCK)],
                xs.at[m, pl.ds(i * BLOCK, BLOCK)],
                sems.at[m, i],
            )
            for i in range(NX)
        ]
        for m in range(2)
    ]
    for m in range(2):
        for i in range(NX):
            copies[m][i].start()
    for m in range(2):
        for i in range(NX):
            copies[m][i].wait()
        for i in range(CHAN // 256):
            xt[i * 256 : (i + 1) * 256, :] = xs[m, :, i * 256 : (i + 1) * 256].T
        for out, core in ((mine, c), (other, 1 - c)):
            for j in range(PLANES):
                row = own_row(j, core)
                row2 = pl.multiple_of(row + AY, 32)
                out[m, j * AY : (j + 1) * AY, :] = xt[pl.ds(row, AY), :]
                start = PLANES * AY + j * BY
                out[m, start : start + BY, :] = xt[pl.ds(row2, BY), :]


def tokens(where, tok):
    half = jax.ShapeDtypeStruct((2, CHAN // 2, TOKENS), bf16)
    return pl.pallas_call(
        token_kernel,
        out_shape=[jax.ShapeDtypeStruct((2, TOKENS, CHAN), bf16), half, half],
        in_specs=[pl.BlockSpec(memory_space=pltpu.SMEM)]
        + [pl.BlockSpec(memory_space=pl.ANY)] * NX,
        out_specs=vmem_specs(3),
        scratch_shapes=[pltpu.VMEM((CHAN, TOKENS), bf16), pltpu.SemaphoreType.DMA((2, NX))],
        compiler_params=pltpu.CompilerParams(vmem_limit_bytes=20 * 2**20),
        cost_estimate=pl.CostEstimate(flops=0, bytes_accessed=12_000_000, transcendentals=0),
        name="tokens",
    )(where, *tok)


def activation_kernel(where, *refs):
    bias, xs = refs[:2]
    first = refs[2:4]
    second = refs[4 : 4 + NY], refs[4 + NY : 4 + 2 * NY]
    act, pre_grad, w_in, w_out, held, sems = refs[4 + 2 * NY :]
    copies = [
        [pltpu.make_async_copy(second[d][r], held.at[d, r], sems.at[d, r]) for r in range(NY)]
        for d in range(2)
    ]
    for d in range(2):
        for r in range(NY):
            copies[d][r].start()
    for d in range(2):
        for k in range(NZ):
            for r in range(NY):
                row, col = place(where, d, k, r)
                for m, w in ((0, w_in), (1, w_out)):
                    w[pl.ds(row, AY), col] = first[d][k, r, m]
    for d in range(2):
        for r in range(NY):
            copies[d][r].wait()
            for k in range(NZ):
                row, col = place(where, d, k, r)
                row2 = pl.multiple_of(row + AY, 32)
                for m, w in ((0, w_in), (1, w_out)):
                    w[pl.ds(row2, BY), col] = held[d, r, k, m]

    width = 256

    def products(i):
        cols = slice(i * width, (i + 1) * width)
        pre = jnp.dot(xs[0], w_in[:, cols], preferred_element_type=f32) + bias[:, cols]
        return pre, jnp.dot(xs[1], w_out[:, cols], preferred_element_type=f32)

    count = HIDDEN // width
    pre, back = products(0)
    for i in range(count):
        following = products(i + 1) if i + 1 < count else None
        cols = slice(i * width, (i + 1) * width)
        cdf = 0.5 * (1.0 + lax.erf(pre * root_half))
        slope = cdf + pre * jnp.exp(-0.5 * pre * pre) * density_norm
        act[:, cols] = (pre * cdf).astype(bf16)
        pre_grad[:, cols] = (back * slope).astype(bf16)
        if following is not None:
            pre, back = following


def activations(where, bias, xs, first, second):
    operands = [bias, xs, *first, *second[0], *second[1]]
    out = jax.ShapeDtypeStruct((TOKENS, HIDDEN), bf16)
    return pl.pallas_call(
        activation_kernel,
        out_shape=[out, out, jax.ShapeDtypeStruct((CHAN, HIDDEN), bf16)],
        in_specs=[pl.BlockSpec(memory_space=pltpu.SMEM)]
        + vmem_specs(4)
        + [pl.BlockSpec(memory_space=pl.ANY)] * (2 * NY),
        out_specs=vmem_specs(3),
        scratch_shapes=[
            pltpu.VMEM((CHAN, HIDDEN), bf16),
            pltpu.VMEM((2, NY, NZ, 2, BY, COLS), bf16),
            pltpu.SemaphoreType.DMA((2, NY)),
        ],
        compiler_params=pltpu.CompilerParams(vmem_limit_bytes=40 * 2**20),
        cost_estimate=pl.CostEstimate(
            flops=4 * TOKENS * CHAN * HIDDEN, bytes_accessed=25_000_000, transcendentals=0
        ),
        name="activations",
    )(where, *operands)


def normed_kernel(pre_grad, w_in, *outs):
    part = lax.dot_general(
        pre_grad[...], w_in[...], (((1,), (1,)), ((), ())), preferred_element_type=f32
    ).astype(bf16)
    for b in range(NX):
        outs[b][...] = part[b * BLOCK : (b + 1) * BLOCK]


def normed_gradient(pre_grad, w_in):
    width = 256
    return pl.pallas_call(
        normed_kernel,
        grid=(CHAN // width,),
        out_shape=[jax.ShapeDtypeStruct((BLOCK, CHAN), bf16)] * NX,
        in_specs=[
            pl.BlockSpec((TOKENS, HIDDEN), lambda i: (0, 0)),
            pl.BlockSpec((width, HIDDEN), lambda i: (i, 0)),
        ],
        out_specs=[pl.BlockSpec((BLOCK, width), lambda i: (0, i))] * NX,
        compiler_params=pltpu.CompilerParams(vmem_limit_bytes=20 * 2**20),
        cost_estimate=pl.CostEstimate(
            flops=2 * TOKENS * CHAN * HIDDEN, bytes_accessed=20_000_000, transcendentals=0
        ),
        name="normed_gradient",
    )(pre_grad, w_in)


def weight_kernel(where, mine, got, *refs):
    sides, (ys, out_z, g) = (refs[0:2], refs[2:4]), (refs[4 : 4 + NY], *refs[4 + NY : 6 + NY])
    held_y, held_z, sems = refs[6 + NY :]
    copies = [
        [
            pltpu.make_async_copy(held_y.at[m, r], ys[r].at[:, m], sems.at[m, r])
            for r in range(NY)
        ]
        + [pltpu.make_async_copy(held_z.at[m], out_z.at[:, :, m], sems.at[m, NY])]
        for m in range(2)
    ]
    width = 256
    for m in range(2):
        own, other = sides[m]

        def step(i, _, m=m, own=own, other=other):
            cols = pl.ds(pl.multiple_of(i * width, width), width)
            value = jnp.dot(mine[m], own[:, cols], preferred_element_type=f32)
            value = value + jnp.dot(got[m], other[:, cols], preferred_element_type=f32)
            g[:, cols] = value.astype(bf16)
            return 0

        lax.fori_loop(0, HIDDEN // width, step, 0)
        for k in range(NZ):
            col = slice(k % 4 * COLS, k % 4 * COLS + COLS)
            for r in range(NY):
                j = k // 4 * NY + lax.rem(where[0] + r, NY)
                row = pl.multiple_of(j * AY, 32)
                row2 = pl.multiple_of(PLANES * AY + j * BY, 32)
                held_z[m, k, r] = g[pl.ds(row, AY), col]
                held_y[m, r, k] = g[pl.ds(row2, BY), col]
        for copy in copies[m]:
            copy.start()
    for m in range(2):
        for copy in copies[m]:
            copy.wait()


def weight_gradients(where, mine, got, pre_grad, other_pre_grad, act, other_act):
    operands = [mine, got, pre_grad, other_pre_grad, act, other_act]
    out = pl.pallas_call(
        weight_kernel,
        out_shape=[jax.ShapeDtypeStruct((NZ, 2, BY, COLS), bf16)] * NY
        + [jax.ShapeDtypeStruct((NZ, NY, 2, AY, COLS), bf16)],
        in_specs=[pl.BlockSpec(memory_space=pltpu.SMEM)] + vmem_specs(len(operands)),
        out_specs=[pl.BlockSpec(memory_space=pltpu.HBM)] * (NY + 1),
        scratch_shapes=[
            pltpu.VMEM((CHAN // 2, HIDDEN), bf16),
            pltpu.VMEM((2, NY, NZ, BY, COLS), bf16),
            pltpu.VMEM((2, NZ, NY, AY, COLS), bf16),
            pltpu.SemaphoreType.DMA((2, NY + 1)),
        ],
        compiler_params=pltpu.CompilerParams(vmem_limit_bytes=32 * 2**20),
        cost_estimate=pl.CostEstimate(
            flops=4 * TOKENS * CHAN * HIDDEN, bytes_accessed=30_000_000, transcendentals=0
        ),
        name="weight_gradients",
    )(where, *operands)
    return out[:NY], out[NY]


def sum_y_kernel(*refs):
    for k in range(NZ):
        total = refs[0][k].astype(f32)
        for ref in refs[1:NY]:
            total = total + ref[k].astype(f32)
        refs[NY][k] = total.astype(bf16)


def sum_y(parts):
    vmem = pl.BlockSpec(memory_space=pltpu.VMEM)
    return pl.pallas_call(
        sum_y_kernel,
        out_shape=jax.ShapeDtypeStruct(parts[0].shape, bf16),
        in_specs=[vmem] * NY,
        out_specs=vmem,
        compiler_params=pltpu.CompilerParams(vmem_limit_bytes=24 * 2**20),
        name="sum_y",
    )(*parts)


def sum_z_kernel(parts, *outs):
    for r in range(NY):
        total = parts[0, r].astype(f32)
        for k in range(1, NZ):
            total = total + parts[k, r].astype(f32)
        outs[r][...] = total.astype(bf16)


def sum_z(parts):
    vmem = pl.BlockSpec(memory_space=pltpu.VMEM)
    return pl.pallas_call(
        sum_z_kernel,
        out_shape=[jax.ShapeDtypeStruct(parts.shape[2:], bf16)] * NY,
        in_specs=[vmem],
        out_specs=[vmem] * NY,
        compiler_params=pltpu.CompilerParams(vmem_limit_bytes=24 * 2**20),
        name="sum_z",
    )(parts)


def finish_kernel(*refs):
    zs, (ys, grad_in, grad_out) = refs[:NY], refs[NY:]
    factor = 1.0 / math.sqrt(BLOCK * 256)
    for m in range(2):
        lead = zs[0][m].astype(f32)
        for part in zs[1:]:
            lead = lead + part[m].astype(f32)
        rest = ys[0, m].astype(f32)
        for k in range(1, NZ):
            rest = rest + ys[k, m].astype(f32)
        value = jnp.concatenate([lead, rest]) * factor
        if m == 0:
            grad_in[...] = value
        else:
            grad_out[...] = value.T


def finish(zs, ys):
    return pl.pallas_call(
        finish_kernel,
        out_shape=[
            jax.ShapeDtypeStruct((ROWS, COLS), f32),
            jax.ShapeDtypeStruct((COLS, ROWS), f32),
        ],
        in_specs=vmem_specs(NY + 1),
        out_specs=vmem_specs(2),
        compiler_params=pltpu.CompilerParams(vmem_limit_bytes=8 * 2**20),
        name="finish",
    )(*zs, ys)


def body(
    conv_out, out_grad, layer_norm_gain, layer_norm_bias, w_in, b_in, w_out, layer_scale, dw_kernel
):
    gain, shift_row, scale = (
        v.reshape(1, CHAN) for v in (layer_norm_gain, layer_norm_bias, layer_scale)
    )
    token, xhat, inverse = layer_norm(
        conv_out.reshape(BLOCK, CHAN), out_grad.reshape(BLOCK, CHAN), gain, shift_row, scale
    )
    tok = [to_x(token, -r) for r in range(NX)]

    shards = jnp.stack([w_in, w_out.T])
    lead, rest = shards[:, :AY], shards[:, AY:]
    got = gather_z(jnp.concatenate([rest.reshape(2 * BY, COLS), bias_rows(b_in)]))
    lead_y = jnp.stack([to_y(lead, -r) for r in range(NY)])
    got, lead_y, tok[1], tok[3] = lax.optimization_barrier((got, lead_y, tok[1], tok[3]))
    rest_z = got[:, : 2 * BY].reshape(NZ, 2, BY, COLS)
    bias = jnp.sum(got[:4, 2 * BY : 2 * BY + 3].astype(f32), axis=1).reshape(1, HIDDEN)
    second = [to_y(rest_z, -r) for r in range(NY)]
    first = gather_z(lead_y)
    swapped = [swap(v) for v in second[:2]] + [None, swap(second[3])]
    where = jnp.stack([lax.axis_index("y"), lax.axis_index("c")]).astype(jnp.int32)
    first, swapped[1], swapped[3], second[2], tok[2] = lax.optimization_barrier(
        (first, swapped[1], swapped[3], second[2], tok[2])
    )
    xs, mine, other = tokens(where, tok)
    other = swap(other)
    swapped[2] = swap(second[2])
    second = [second, swapped]
    first = [first, swap(first)]

    act, pre_grad, w_all = activations(where, bias, xs, first, second)
    other_act, other_pre_grad = swap(act), swap(pre_grad)
    part = normed_gradient(pre_grad, w_all)
    other_act, other_pre_grad, *part = lax.optimization_barrier(
        (other_act, other_pre_grad, *part)
    )
    part = [to_x(v, r) for r, v in enumerate(part)]
    ys, zs = weight_gradients(where, mine, other, pre_grad, other_pre_grad, act, other_act)
    zs, part[1], part[3] = lax.optimization_barrier((zs, part[1], part[3]))
    ys = [to_y(v, r) for r, v in enumerate(ys)]
    own, first_cols, last_cols = layer_norm_backward(part, xhat, inverse, gain)
    left, right = to_tile(last_cols, 0, 1), to_tile(first_cols, 0, -1)
    first_rows, last_rows = edges(own, left, right)
    up, down = to_tile(last_rows, 1, 0), to_tile(first_rows, -1, 0)
    ys = sum_y(ys)
    ys, up, down = lax.optimization_barrier((ys, up, down))
    zs = sum_z(exchange_z(zs))
    own, *zs = lax.optimization_barrier((own, *zs))
    zs = [to_y(v, r) for r, v in enumerate(zs)]
    ys = exchange_z(ys)
    grad_input = convolution(own, left, right, up, down, dw_kernel, out_grad)
    grad_input, ys = lax.optimization_barrier((grad_input, ys))
    grad_in, grad_out = finish(zs, ys)
    return (grad_input, grad_in, grad_out)


def solution(mesh):
    fine = Mesh(mesh.devices.reshape(SIZES), FINE)
    token = P(STRIP, TENSOR, None)
    return jax.shard_map(
        body,
        mesh=fine,
        in_specs=(
            token,
            token,
            P(),
            P(),
            P(STRIP, TENSOR),
            P(TENSOR),
            P(TENSOR, STRIP),
            P(),
            P(),
        ),
        out_specs=(token, P(STRIP, TENSOR), P(TENSOR, STRIP)),
        check_vma=False,
    )
```
